32 devices in a mesh: row: 4 (over z), col: 4 (over y, core), rep: 2 (over x).
Axes of the slice: x: 2, y: 2, z: 4, core: 2. Of those that a mesh axis runs over, the one named last changes fastest.
Arguments:
- queries: bfloat16 [16384, 768], P(('rep', 'row', 'col')), parts along dimension 0, may hold values from -16 to 16
- passages: bfloat16 [12288, 768], P(('rep', 'row', 'col')), parts along dimension 0, may hold values from -16 to 16
- positive: int32 [16384], P(('rep', 'row', 'col')), parts along dimension 0, may hold values from 0 to 383
- block_mask: int32 [16384, 9], P(('rep', 'row', 'col')), parts along dimension 0, may hold values from 0 to 1
- roster: int32 [16384, 3], P(('rep', 'row', 'col')), parts along dimension 0, may hold values from 0 to 2
Outputs:
- loss: float32 [2], P('rep'), parts along dimension 0
- grad_queries: float32 [16384, 768], P(('rep', 'row', 'col')), parts along dimension 0
- grad_passages: float32 [12288, 768], P(('rep', 'row', 'col')), parts along dimension 0
The draws below stay inside these ranges and needn't reach their ends.
There are 2 independent parts, one for each index of `rep`. The reference program is written for one: setup_inputs(seed, part) draws one part's arguments, and reference() takes and returns one part's arrays. A program takes and returns all parts, laid end to end along the dimension named above; each array names one. Nothing has to cross between parts.
All inputs are finite; a program needn't handle non-finite values.
Results may differ from the reference program's by a relative error of at most 0.002.
Values may be sent and summed in bfloat16 or wider, within the bound.
No kernel may reach another device: no remote copies, remote signals or barrier semaphores. Data moves between devices by JAX's collectives and lax.ppermute only.
A program may use at most 128 MiB of HBM per device.

```python
import math
import jax
import jax.numpy as jnp
from jax import lax

D = 768
Q_DEV = 512
P_DEV = 384
BLK = 128
PB = 3
REACH = 1
NB = 9
QN = 8192
PN = 6144
N_ROW = 4
N_COL = 4


def positive_rows(key):
    return jax.random.randint(jax.random.fold_in(key, 7), (QN,), 0, P_DEV, dtype=jnp.int32)


def embedding_pair(key):
    keys = [jax.random.fold_in(key, 100 + number) for number in range(8)]
    base_q = jnp.clip(jax.random.normal(keys[0], (QN, D), jnp.float32), -4.0, 4.0)
    base_p = jnp.clip(jax.random.normal(keys[1], (PN, D), jnp.float32), -4.0, 4.0)
    scale_q = jnp.exp(jax.random.uniform(keys[2], (QN, 1), jnp.float32, math.log(0.3), math.log(3.0)))
    scale_p = jnp.exp(jax.random.uniform(keys[3], (PN, 1), jnp.float32, math.log(0.3), math.log(3.0)))
    queries = scale_q * base_q
    passages = scale_p * base_p
    return (queries, passages)


def draw_queries(key, part):
    return embedding_pair(key)[0].astype(jnp.bfloat16)


def draw_passages(key, part):
    return embedding_pair(key)[1].astype(jnp.bfloat16)


def draw_positive(key, part):
    return positive_rows(key)


def draw_block_mask(key, part):
    cells = QN // Q_DEV
    level = jax.random.randint(jax.random.fold_in(key, 21), (cells, 1, 1), 1, 5, dtype=jnp.int32)
    alive = jax.random.randint(jax.random.fold_in(key, 22), (cells, 1, NB), 0, 4, dtype=jnp.int32) < level
    coins = jax.random.randint(jax.random.fold_in(key, 23), (cells, Q_DEV, NB), 0, 2, dtype=jnp.int32)
    return (coins * alive.astype(jnp.int32)).reshape(QN, NB)


def place_ends(array, own_key, smallest, top_value):
    longest = array.shape.index(max(array.shape))
    spots = []
    for shift in (0, 1):
        where = [jax.random.randint(jax.random.fold_in(own_key, axis), (), 0, length) for axis, length in enumerate(array.shape)]
        where[longest] = (where[longest] + shift) % array.shape[longest]
        spots.append(tuple(where))
    return array.at[spots[0]].set(smallest).at[spots[1]].set(top_value)


def setup_inputs(seed: int = 0, part: int = 0) -> dict:
    streams_of = jax.random.split(jax.random.key(seed), 6)
    part_keys = jax.random.split(jax.random.fold_in(streams_of[5], part), 6)
    queries = draw_queries(jax.random.fold_in(jax.random.fold_in(streams_of[5], part), 71), part)
    passages = draw_passages(jax.random.fold_in(jax.random.fold_in(streams_of[5], part), 71), part)
    positive = draw_positive(jax.random.fold_in(jax.random.fold_in(streams_of[5], part), 71), part)
    block_mask = draw_block_mask(jax.random.fold_in(jax.random.fold_in(streams_of[5], part), 71), part)
    roster = place_ends(jax.random.randint(part_keys[4], (QN, N_COL - 1), 0, PB), jax.random.fold_in(part_keys[4], 1), 0, PB - 1).astype(jnp.int32)
    return {"queries": queries, "passages": passages, "positive": positive, "block_mask": block_mask, "roster": roster}


def visited_cells(cell_at):
    row_at = cell_at // N_COL
    col_at = cell_at % N_COL
    listed = [cell_at]
    for offset in list(range(-REACH, 0)) + list(range(1, REACH + 1)):
        listed.append(((row_at + offset) % N_ROW) * N_COL + col_at)
    for stride in range(1, N_COL):
        listed.append(row_at * N_COL + (col_at - stride) % N_COL)
    return listed


def reference(queries, passages, positive, block_mask, roster):
    scale = D ** -0.5
    block_ids = jnp.arange(P_DEV, dtype=jnp.int32) // BLK
    group_count = N_COL + 2 * REACH
    column_all = jnp.arange(group_count * P_DEV, dtype=jnp.int32)

    def one_cell(carried, cell_at):
        grad_rows, loss_sum = carried
        first = (cell_at * Q_DEV).astype(jnp.int32)
        query_rows = lax.dynamic_slice_in_dim(queries, first, Q_DEV, 0)
        targets = lax.dynamic_slice_in_dim(positive, first, Q_DEV, 0)
        masks_here = lax.dynamic_slice_in_dim(block_mask, first, Q_DEV, 0)
        plans_here = lax.dynamic_slice_in_dim(roster, first, Q_DEV, 0)
        visited = visited_cells(cell_at)
        cell_rows = jnp.concatenate([lax.dynamic_slice_in_dim(passages, (other * P_DEV).astype(jnp.int32), P_DEV, 0) for other in visited], axis=0)
        parts_seen = [(jnp.repeat(masks_here[:, 0:PB], BLK, axis=1) == 1) | (block_ids[None, :] == (targets // BLK)[:, None])]
        for group_at in range(1, 2 * REACH + 1):
            parts_seen.append(jnp.repeat(masks_here[:, group_at * PB:(group_at + 1) * PB], BLK, axis=1) == 1)
        for stride in range(1, N_COL):
            parts_seen.append(block_ids[None, :] == plans_here[:, stride - 1:stride])
        visible = jnp.concatenate(parts_seen, axis=1)
        scores = jnp.dot(query_rows, cell_rows.T, preferred_element_type=jnp.float32) * scale
        highest = jnp.max(jnp.where(visible, scores, -jnp.inf), axis=1)
        summed = jnp.sum(jnp.where(visible, jnp.exp(scores - highest[:, None]), 0.0), axis=1)
        log_total = highest + jnp.log(summed)
        target_mask = column_all[None, :] == targets[:, None]
        positive_score = jnp.sum(jnp.where(target_mask, scores, 0.0), axis=1)
        weights = jnp.where(visible, jnp.exp(scores - log_total[:, None]), 0.0) - target_mask.astype(jnp.float32)
        weights = weights.astype(jnp.bfloat16)
        toward = jnp.dot(weights, cell_rows, preferred_element_type=jnp.float32) * scale
        pieces = lax.dot_general(weights, query_rows, (((0,), (0,)), ((), ())), preferred_element_type=jnp.float32) * scale
        for group_at, other in enumerate(visited):
            start = (other * P_DEV).astype(jnp.int32)
            former = lax.dynamic_slice_in_dim(grad_rows, start, P_DEV, 0)
            grad_rows = lax.dynamic_update_slice_in_dim(grad_rows, former + pieces[group_at * P_DEV:(group_at + 1) * P_DEV], start, 0)
        loss_sum = loss_sum + jnp.sum(log_total - positive_score)
        return (grad_rows, loss_sum), toward

    initial = (jnp.zeros((PN, D), jnp.float32), jnp.zeros((), jnp.float32))
    (grad_passages, loss_sum), towards = lax.scan(one_cell, initial, jnp.arange(N_ROW * N_COL, dtype=jnp.int32))
    return (loss_sum / QN).reshape(1), towards.reshape(QN, D), grad_passages
```

```python
import functools
import math

import jax
import jax.numpy as jnp
from jax import lax
from jax.experimental import pallas as pl
from jax.experimental.pallas import tpu as pltpu
from jax.sharding import PartitionSpec as P

BLK = 128
LOWEST = -1e30
LOG2E = math.log2(math.e)
VMEM_LIMIT = 24 << 20


def whole():
    return pl.BlockSpec(memory_space=pltpu.VMEM)


def call(kernel, name, outs, ins, flops, exps=0):
    moved = sum(a.size * a.dtype.itemsize for a in (*outs, *ins))
    return pl.pallas_call(
        kernel,
        name=name,
        out_shape=tuple(outs),
        in_specs=[whole() for _ in ins],
        out_specs=tuple(whole() for _ in outs),
        compiler_params=pltpu.CompilerParams(vmem_limit_bytes=VMEM_LIMIT),
        cost_estimate=pl.CostEstimate(flops=flops, bytes_accessed=moved, transcendentals=exps),
    )(*ins)


def send(array, axis, pairs):
    return lax.ppermute(array, axis, pairs)


def block_stats(scores, block_at, scale):
    part = scores[block_at * BLK : (block_at + 1) * BLK]
    highest = jnp.max(part, axis=0, keepdims=True)
    raised = jnp.exp2((part - highest) * (scale * LOG2E))
    return part, highest, raised, jnp.sum(raised, axis=0, keepdims=True)


def scores_of(q_ref, p_ref):
    return lax.dot_general(
        p_ref[...], q_ref[...], (((1,), (1,)), ((), ())), preferred_element_type=jnp.float32
    )


def scores_body(scale, blocks, own, *refs):
    if own:
        q_ref, p_ref, pos_ref, e_ref, stats_ref = refs
    else:
        q_ref, p_ref, e_ref, stats_ref = refs
    scores = scores_of(q_ref, p_ref)
    stats_ref[...] = jnp.zeros_like(stats_ref)
    picked = None
    for block_at in range(blocks):
        part, highest, raised, summed = block_stats(scores, block_at, scale)
        e_ref[block_at * BLK : (block_at + 1) * BLK, :] = raised
        stats_ref[block_at : block_at + 1, :] = highest * scale
        stats_ref[blocks + block_at : blocks + block_at + 1, :] = summed
        if own:
            rows = lax.broadcasted_iota(jnp.int32, part.shape, 0) + block_at * BLK
            hit = jnp.sum(jnp.where(rows == pos_ref[...], part, 0.0), axis=0, keepdims=True)
            picked = hit if picked is None else picked + hit
    if own:
        stats_ref[2 * blocks : 2 * blocks + 1, :] = picked * scale


def weights_of(e_ref, f, blocks, pos):
    parts = []
    for block_at in range(blocks):
        part = e_ref[block_at * BLK : (block_at + 1) * BLK, :] * f[block_at : block_at + 1, :]
        if pos is not None:
            rows = lax.broadcasted_iota(jnp.int32, part.shape, 0) + block_at * BLK
            part = part - jnp.where(rows == pos, 1.0, 0.0)
        parts.append(part.astype(jnp.bfloat16))
    return jnp.concatenate(parts, axis=0)


def last_body(scale, blocks, cells, first, *refs):
    q_ref, p_ref, e_first_ref, vis_ref = refs[:4]
    stats_refs = refs[4 : 4 + cells - 1]
    e_ref, f_ref, g_ref, w_ref, loss_ref = refs[4 + cells - 1 :]
    scores = scores_of(q_ref, p_ref)
    tops, sums = [], []
    for block_at in range(blocks):
        _, highest, raised, summed = block_stats(scores, block_at, scale)
        e_ref[block_at * BLK : (block_at + 1) * BLK, :] = raised
        tops.append(highest * scale)
        sums.append(summed)
    all_tops = [s[0:blocks, :] for s in stats_refs] + [jnp.concatenate(tops, axis=0)]
    all_sums = [s[blocks : 2 * blocks, :] for s in stats_refs] + [jnp.concatenate(sums, axis=0)]
    seen = [vis_ref[cell * 8 : cell * 8 + blocks, :] > 0 for cell in range(cells)]
    highest = None
    for cell in range(cells):
        top = jnp.max(jnp.where(seen[cell], all_tops[cell], LOWEST), axis=0, keepdims=True)
        highest = top if highest is None else jnp.maximum(highest, top)
    total = None
    for cell in range(cells):
        gap = jnp.where(seen[cell], all_tops[cell] - highest, LOWEST)
        part = jnp.sum(all_sums[cell] * jnp.exp(gap), axis=0, keepdims=True)
        total = part if total is None else total + part
    log_total = highest + jnp.log(total)
    factors = []
    f_ref[...] = jnp.zeros_like(f_ref)
    for cell in range(cells):
        factor = jnp.exp(jnp.where(seen[cell], all_tops[cell] - log_total, LOWEST))
        f_ref[cell * 8 : cell * 8 + blocks, :] = factor
        factors.append(factor)
    positive_score = stats_refs[0][2 * blocks : 2 * blocks + 1, :]
    lost = jnp.sum(log_total - positive_score, axis=1, keepdims=True)
    loss_ref[...] = jnp.broadcast_to(lost, loss_ref.shape)
    weights = weights_of(e_first_ref, factors[first], blocks, None)
    w_ref[...] = weights
    gradient = jnp.dot(weights, q_ref[...], preferred_element_type=jnp.float32) * scale
    g_ref[...] = gradient.astype(g_ref.dtype)


def gradient_body(scale, blocks, cell, own, added, *refs):
    refs = list(refs)
    q_ref, e_ref, f_ref = refs[:3]
    del refs[:3]
    pos = refs.pop(0)[...] if own else None
    more_ref = refs.pop(0) if added else None
    g_ref, w_ref = refs
    weights = weights_of(e_ref, f_ref[cell * 8 : cell * 8 + 8, :], blocks, pos)
    w_ref[...] = weights
    gradient = jnp.dot(weights, q_ref[...], preferred_element_type=jnp.float32) * scale
    if added:
        gradient = gradient + more_ref[...].astype(jnp.float32)
    g_ref[...] = gradient.astype(g_ref.dtype)


def toward_body(scale, cells, *refs):
    w_refs, p_refs, out_ref = refs[:cells], refs[cells : 2 * cells], refs[2 * cells]
    total = None
    for w_ref, p_ref in zip(w_refs, p_refs):
        part = lax.dot_general(
            w_ref[...], p_ref[...], (((0,), (0,)), ((), ())), preferred_element_type=jnp.float32
        )
        total = part if total is None else total + part
    out_ref[...] = total * scale


def row_plan(n_row, reach):
    plan = []
    if reach == 1 and n_row % 2 == 0:
        even_up = [(i, i ^ 1) for i in range(n_row)]
        odd_up = [(i, (i + 1) % n_row if i % 2 else (i - 1) % n_row) for i in range(n_row)]
        plan.append((even_up, even_up, (2, 1)))
        plan.append((odd_up, odd_up, (1, 2)))
        return plan
    offsets = list(range(-reach, 0)) + list(range(1, reach + 1))
    for group_at, offset in enumerate(offsets):
        there = [((i + offset) % n_row, i) for i in range(n_row)]
        back = [(i, (i + offset) % n_row) for i in range(n_row)]
        plan.append((there, back, (group_at + 1, group_at + 1)))
    return plan


def sum_over(array, axis):
    size = lax.axis_size(axis)
    if size & (size - 1):
        return lax.psum(array, axis)
    step = 1
    while step < size:
        array = array + send(array, axis, [(i, i ^ step) for i in range(size)])
        step *= 2
    return array


def local(queries, passages, positive, block_mask, roster):
    n_row = lax.axis_size("row")
    n_col = lax.axis_size("col")
    reach = min(2, (n_row - 1) // 2)
    count, width = queries.shape
    held = passages.shape[0]
    blocks = held // BLK
    scale = width ** (-0.5)
    odd_row = lax.axis_index("row") % 2 == 1
    odd_col = lax.axis_index("col") % 2 == 1
    f32, bf16 = jnp.float32, jnp.bfloat16

    rows = row_plan(n_row, reach)
    near = [send(passages, "row", there) for there, _, _ in rows]

    swap = [(i, i ^ 1) for i in range(n_col)]
    col_cells = []
    paired = n_col % 2 == 0
    if paired:
        col_cells.append((send(passages, "col", swap), 1, n_col - 1))
        for apart in range(1, n_col // 2):
            far = send(passages, "col", [(i, (i + 2 * apart) % n_col) for i in range(n_col)])
            cross = send(far, "col", swap)
            col_cells.append((far, 2 * apart, 2 * apart))
            col_cells.append((cross, 2 * apart + 1, 2 * apart - 1))
    else:
        for stride in range(1, n_col):
            far = send(passages, "col", [(i, (i + stride) % n_col) for i in range(n_col)])
            col_cells.append((far, stride, stride))

    mask_t = block_mask.T
    roster_t = roster.T
    pos = positive.reshape(1, count)
    ids = jnp.arange(blocks, dtype=jnp.int32)[:, None]
    pad = jnp.zeros((8 - blocks, count), f32)

    def padded(flags):
        return jnp.concatenate([flags.astype(f32), pad], axis=0)

    def group_rows(group):
        return mask_t[group * blocks : (group + 1) * blocks] == 1

    seen = [padded(group_rows(0) | (pos // BLK == ids))]
    for _, odd, even in col_cells:
        seen.append(
            padded(jnp.where(odd_col, roster_t[odd - 1][None], roster_t[even - 1][None]) == ids)
        )
    for _, _, (even, odd) in rows:
        seen.append(padded(jnp.where(odd_row, group_rows(odd), group_rows(even))))
    vis = jnp.concatenate(seen, axis=0)

    cell_rows = [passages] + [cell[0] for cell in col_cells] + near
    cells = len(cell_rows)
    e_shape = jax.ShapeDtypeStruct((held, count), f32)
    w_shape = jax.ShapeDtypeStruct((held, count), bf16)
    s_shape = jax.ShapeDtypeStruct((8, count), f32)
    g_wire = jax.ShapeDtypeStruct((held, width), bf16)
    g_wide = jax.ShapeDtypeStruct((held, width), f32)
    dot_flops = 2 * held * count * width

    raised, stats = [], []
    for cell in range(cells - 1):
        own = cell == 0
        ins = (queries, cell_rows[cell]) + ((pos,) if own else ())
        e, s = call(
            functools.partial(scores_body, scale, blocks, own),
            f"scores_{cell}",
            (e_shape, s_shape),
            ins,
            dot_flops,
            held * count,
        )
        raised.append(e)
        stats.append(s)

    first = cells - len(rows)
    last = cells - 1
    f_shape = jax.ShapeDtypeStruct((8 * cells, count), f32)
    loss_shape = jax.ShapeDtypeStruct((8, BLK), f32)
    e, factors, g_first, w_first, lost = call(
        functools.partial(last_body, scale, blocks, cells, first),
        "last",
        (e_shape, f_shape, g_wire, w_shape, loss_shape),
        (queries, cell_rows[last], raised[first], vis, *stats),
        2 * dot_flops,
        held * count,
    )
    raised.append(e)
    weights = {first: w_first}

    def gradient_of(cell, shape, added=None):
        own = cell == 0
        ins = (queries, raised[cell], factors)
        ins += ((pos,) if own else ()) + (() if added is None else (added,))
        g, w = call(
            functools.partial(gradient_body, scale, blocks, cell, own, added is not None),
            f"gradient_{cell}",
            (shape, w_shape),
            ins,
            dot_flops,
        )
        weights[cell] = w
        return g

    returned = []
    for at, (_, back, _) in enumerate(rows):
        g = g_first if at == 0 else gradient_of(first + at, g_wire)
        returned.append(send(g, "row", back))

    if paired:
        handed = []
        for apart in range(1, n_col // 2):
            handed.append(send(gradient_of(1 + 2 * apart, g_wire), "col", swap))
        for apart in range(1, n_col // 2):
            g = gradient_of(2 * apart, g_wire, handed[apart - 1])
            back = [(i, (i - 2 * apart) % n_col) for i in range(n_col)]
            returned.append(send(g, "col", back))
        returned.append(send(gradient_of(1, g_wire), "col", swap))
    else:
        for stride in range(1, n_col):
            back = [(i, (i - stride) % n_col) for i in range(n_col)]
            returned.append(send(gradient_of(stride, g_wire), "col", back))
    g_own = gradient_of(0, g_wide)

    (toward,) = call(
        functools.partial(toward_body, scale, cells),
        "toward",
        (jax.ShapeDtypeStruct((count, width), f32),),
        (*[weights[cell] for cell in range(cells)], *cell_rows),
        cells * dot_flops,
    )

    loss_total = sum_over(sum_over(lost, "col"), "row")
    loss = loss_total[0, :1] / (count * n_row * n_col)

    near_count = len(rows)
    grad_passages = g_own
    for g in returned[near_count:] + returned[:near_count]:
        grad_passages = grad_passages + g.astype(f32)
    return (loss, toward, grad_passages)


def solution(mesh):
    return jax.shard_map(
        local,
        mesh=mesh,
        in_specs=(
            P(("rep", "row", "col"), None),
            P(("rep", "row", "col"), None),
            P(("rep", "row", "col")),
            P(("rep", "row", "col"), None),
            P(("rep", "row", "col"), None),
        ),
        out_specs=(P("rep"), P(("rep", "row", "col"), None), P(("rep", "row", "col"), None)),
        check_vma=False,
    )
```

```python
import functools
import math

import jax
import jax.numpy as jnp
from jax import lax
from jax.experimental import pallas as pl
from jax.experimental.pallas import tpu as pltpu
from jax.sharding import PartitionSpec as P


BLK = 128
LOWEST = -1e30
LOG2E = math.log2(math.e)
VMEM_LIMIT = 24 << 20
CHUNKS = 4


def whole():
    return pl.BlockSpec(memory_space=pltpu.VMEM)


def call(kernel, outs, ins, flops, exps=0, out_specs=None, scratch=()):
    moved = sum(a.size * a.dtype.itemsize for a in (*outs, *ins))
    return pl.pallas_call(
        kernel,
        out_shape=tuple(outs),
        in_specs=[whole() for _ in ins],
        out_specs=out_specs or tuple(whole() for _ in outs),
        scratch_shapes=scratch,
        compiler_params=pltpu.CompilerParams(vmem_limit_bytes=VMEM_LIMIT),
        cost_estimate=pl.CostEstimate(flops=flops, bytes_accessed=moved, transcendentals=exps),
    )(*ins)


def block_stats(scores, block_at, scale):
    part = scores[block_at * BLK : (block_at + 1) * BLK]
    highest = jnp.max(part, axis=0, keepdims=True)
    raised = jnp.exp2((part - highest) * (scale * LOG2E))
    return part, highest, raised, jnp.sum(raised, axis=0, keepdims=True)


def scores_of(q_ref, p_ref):
    return lax.dot_general(
        p_ref[...], q_ref[...], (((1,), (1,)), ((), ())), preferred_element_type=jnp.float32
    )


def scores_body(scale, blocks, own, *refs):
    if own:
        q_ref, p_ref, pos_ref, e_ref, stats_ref = refs
    else:
        q_ref, p_ref, e_ref, stats_ref = refs
    scores = scores_of(q_ref, p_ref)
    stats_ref[...] = jnp.zeros_like(stats_ref)
    picked = None
    for block_at in range(blocks):
        part, highest, raised, summed = block_stats(scores, block_at, scale)
        e_ref[block_at * BLK : (block_at + 1) * BLK, :] = raised
        stats_ref[block_at : block_at + 1, :] = highest * scale
        stats_ref[blocks + block_at : blocks + block_at + 1, :] = summed
        if own:
            rows = lax.broadcasted_iota(jnp.int32, part.shape, 0) + block_at * BLK
            hit = jnp.sum(jnp.where(rows == pos_ref[...], part, 0.0), axis=0, keepdims=True)
            picked = hit if picked is None else picked + hit
    if own:
        stats_ref[2 * blocks : 2 * blocks + 1, :] = picked * scale


def weights_of(e_ref, f, blocks, pos):
    parts = []
    for block_at in range(blocks):
        part = e_ref[block_at * BLK : (block_at + 1) * BLK, :] * f[block_at : block_at + 1, :]
        if pos is not None:
            rows = lax.broadcasted_iota(jnp.int32, part.shape, 0) + block_at * BLK
            part = part - jnp.where(rows == pos, 1.0, 0.0)
        parts.append(part.astype(jnp.bfloat16))
    return jnp.concatenate(parts, axis=0)


def last_body(scale, blocks, cells, first, *refs):
    q_ref, p_ref, e_first_ref, vis_ref = refs[:4]
    stats_refs = refs[4 : 4 + cells - 1]
    e_ref, f_ref, g_ref, w_ref, loss_ref = refs[4 + cells - 1 :]
    scores = scores_of(q_ref, p_ref)
    tops, sums = [], []
    for block_at in range(blocks):
        _, highest, raised, summed = block_stats(scores, block_at, scale)
        e_ref[block_at * BLK : (block_at + 1) * BLK, :] = raised
        tops.append(highest * scale)
        sums.append(summed)
    all_tops = [s[0:blocks, :] for s in stats_refs] + [jnp.concatenate(tops, axis=0)]
    all_sums = [s[blocks : 2 * blocks, :] for s in stats_refs] + [jnp.concatenate(sums, axis=0)]
    seen = [vis_ref[cell * 8 : cell * 8 + blocks, :] > 0 for cell in range(cells)]
    highest = None
    for cell in range(cells):
        top = jnp.max(jnp.where(seen[cell], all_tops[cell], LOWEST), axis=0, keepdims=True)
        highest = top if highest is None else jnp.maximum(highest, top)
    total = None
    for cell in range(cells):
        gap = jnp.where(seen[cell], all_tops[cell] - highest, LOWEST)
        part = jnp.sum(all_sums[cell] * jnp.exp(gap), axis=0, keepdims=True)
        total = part if total is None else total + part
    log_total = highest + jnp.log(total)
    factors = []
    f_ref[...] = jnp.zeros_like(f_ref)
    for cell in range(cells):
        factor = jnp.exp(jnp.where(seen[cell], all_tops[cell] - log_total, LOWEST))
        f_ref[cell * 8 : cell * 8 + blocks, :] = factor
        factors.append(factor)
    positive_score = stats_refs[0][2 * blocks : 2 * blocks + 1, :]
    lost = jnp.sum(log_total - positive_score, axis=1, keepdims=True)
    loss_ref[...] = jnp.broadcast_to(lost, loss_ref.shape)
    weights = weights_of(e_first_ref, factors[first], blocks, None)
    w_ref[...] = weights
    gradient = jnp.dot(weights, q_ref[...], preferred_element_type=jnp.float32) * scale
    g_ref[...] = gradient.astype(g_ref.dtype)


def gradient_body(scale, blocks, cell, own, added, *refs):
    refs = list(refs)
    q_ref, e_ref, f_ref = refs[:3]
    del refs[:3]
    pos = refs.pop(0)[...] if own else None
    more_ref = refs.pop(0) if added else None
    g_ref, w_ref = refs
    weights = weights_of(e_ref, f_ref[cell * 8 : cell * 8 + 8, :], blocks, pos)
    w_ref[...] = weights
    gradient = jnp.dot(weights, q_ref[...], preferred_element_type=jnp.float32) * scale
    if added:
        gradient = gradient + more_ref[...].astype(jnp.float32)
    g_ref[...] = gradient.astype(g_ref.dtype)


def toward_body(scale, cells, *refs):
    w_refs, p_refs, out_ref = refs[:cells], refs[cells : 2 * cells], refs[2 * cells]
    total = None
    for w_ref, p_ref in zip(w_refs, p_refs):
        part = lax.dot_general(
            w_ref[...], p_ref[...], (((0,), (0,)), ((), ())), preferred_element_type=jnp.float32
        )
        total = part if total is None else total + part
    out_ref[...] = total * scale


def gather_body(*refs):
    total = refs[0][...]
    for ref in refs[1:-1]:
        total = total + ref[...].astype(jnp.float32)
    refs[-1][...] = total


def final_body(share, parts, base_ref, more_ref, *refs):
    lost_refs = refs[:parts]
    loss_ref, out_ref, held_ref, sem = refs[parts:]
    chunk = held_ref.shape[0] // CHUNKS
    copies = []
    for at in range(CHUNKS):
        rows = pl.ds(at * chunk, chunk)
        held_ref[rows, :] = base_ref[rows, :] + more_ref[rows, :].astype(jnp.float32)
        copy = pltpu.make_async_copy(held_ref.at[rows, :], out_ref.at[rows, :], sem.at[at])
        copy.start()
        copies.append(copy)
    total = lost_refs[0][...]
    for ref in lost_refs[1:]:
        total = total + ref[...]
    loss_ref[0] = jnp.max(total) * share
    for copy in copies:
        copy.wait()


def row_plan(n_row, reach):
    plan = []
    if reach == 1 and n_row % 2 == 0:
        even_up = [(i, i ^ 1) for i in range(n_row)]
        odd_up = [(i, (i + 1) % n_row if i % 2 else (i - 1) % n_row) for i in range(n_row)]
        plan.append((even_up, even_up, (2, 1)))
        plan.append((odd_up, odd_up, (1, 2)))
        return plan
    offsets = list(range(-reach, 0)) + list(range(1, reach + 1))
    for group_at, offset in enumerate(offsets):
        there = [((i + offset) % n_row, i) for i in range(n_row)]
        back = [(i, (i + offset) % n_row) for i in range(n_row)]
        plan.append((there, back, (group_at + 1, group_at + 1)))
    return plan


def sum_steps(array, axis):
    size = lax.axis_size(axis)
    if size & (size - 1):
        return lax.psum(array, axis)
    step = 1
    while step < size:
        pairs = [(i, i ^ step) for i in range(size)]
        array = array + lax.ppermute(array, axis, pairs)
        step *= 2
    return array


def from_all(array, axis):
    size = lax.axis_size(axis)
    if size > 4:
        return [sum_steps(array, axis)]
    shifts = range(1, size)
    return [array] + [
        lax.ppermute(array, axis, [(i, (i + s) % size) for i in range(size)]) for s in shifts
    ]


def local_loss(queries, passages, positive, block_mask, roster):
    n_row = lax.axis_size("row")
    n_col = lax.axis_size("col")
    reach = min(2, (n_row - 1) // 2)
    count, width = queries.shape
    held = passages.shape[0]
    blocks = held // BLK
    scale = width ** (-0.5)
    odd_row = lax.axis_index("row") % 2 == 1
    odd_col = lax.axis_index("col") % 2 == 1
    f32, bf16 = jnp.float32, jnp.bfloat16

    rows = row_plan(n_row, reach)
    near = [lax.ppermute(passages, "row", there) for there, _, _ in rows]

    swap = [(i, i ^ 1) for i in range(n_col)]
    col_cells = []
    paired = n_col % 2 == 0
    if paired:
        col_cells.append((lax.ppermute(passages, "col", swap), 1, n_col - 1))
        for apart in range(1, n_col // 2):
            there = [(i, (i + 2 * apart) % n_col) for i in range(n_col)]
            far = lax.ppermute(passages, "col", there)
            cross = lax.ppermute(far, "col", swap)
            col_cells.append((far, 2 * apart, 2 * apart))
            col_cells.append((cross, 2 * apart + 1, 2 * apart - 1))
    else:
        for stride in range(1, n_col):
            there = [(i, (i + stride) % n_col) for i in range(n_col)]
            far = lax.ppermute(passages, "col", there)
            col_cells.append((far, stride, stride))

    mask_t = block_mask.T
    roster_t = roster.T
    pos = positive.reshape(1, count)
    ids = jnp.arange(blocks, dtype=jnp.int32)[:, None]
    pad = jnp.zeros((8 - blocks, count), f32)

    def padded(flags):
        return jnp.concatenate([flags.astype(f32), pad], axis=0)

    def group_rows(group):
        return mask_t[group * blocks : (group + 1) * blocks] == 1

    seen = [padded(group_rows(0) | (pos // BLK == ids))]
    for _, odd, even in col_cells:
        seen.append(
            padded(jnp.where(odd_col, roster_t[odd - 1][None], roster_t[even - 1][None]) == ids)
        )
    for _, _, (even, odd) in rows:
        seen.append(padded(jnp.where(odd_row, group_rows(odd), group_rows(even))))
    vis = jnp.concatenate(seen, axis=0)

    cell_rows = [passages] + [cell[0] for cell in col_cells] + near
    cells = len(cell_rows)
    e_shape = jax.ShapeDtypeStruct((held, count), f32)
    w_shape = jax.ShapeDtypeStruct((held, count), bf16)
    s_shape = jax.ShapeDtypeStruct((8, count), f32)
    g_wire = jax.ShapeDtypeStruct((held, width), bf16)
    g_wide = jax.ShapeDtypeStruct((held, width), f32)
    dot_flops = 2 * held * count * width

    raised, stats = [], []
    for cell in range(cells - 1):
        own = cell == 0
        ins = (queries, cell_rows[cell]) + ((pos,) if own else ())
        e, s = call(
            functools.partial(scores_body, scale, blocks, own),
            (e_shape, s_shape),
            ins,
            dot_flops,
            held * count,
        )
        raised.append(e)
        stats.append(s)

    first = cells - len(rows)
    last = cells - 1
    f_shape = jax.ShapeDtypeStruct((8 * cells, count), f32)
    loss_shape = jax.ShapeDtypeStruct((8, BLK), f32)
    e, factors, g_first, w_first, lost = call(
        functools.partial(last_body, scale, blocks, cells, first),
        (e_shape, f_shape, g_wire, w_shape, loss_shape),
        (queries, cell_rows[last], raised[first], vis, *stats),
        2 * dot_flops,
        held * count,
    )
    raised.append(e)
    weights = {first: w_first}

    def gradient_of(cell, shape, added=None):
        own = cell == 0
        ins = (queries, raised[cell], factors)
        ins += ((pos,) if own else ()) + (() if added is None else (added,))
        g, w = call(
            functools.partial(gradient_body, scale, blocks, cell, own, added is not None),
            (shape, w_shape),
            ins,
            dot_flops,
        )
        weights[cell] = w
        return g

    near_back = []
    for at, (_, back, _) in enumerate(rows):
        g = g_first if at == 0 else gradient_of(first + at, g_wire)
        near_back.append(lax.ppermute(g, "row", back))

    lost_col = sum_steps(lost, "col")
    lost_parts = from_all(lost_col, "row")

    col_back = []
    if paired:
        handed = []
        for apart in range(1, n_col // 2):
            g = gradient_of(1 + 2 * apart, g_wire)
            handed.append(lax.ppermute(g, "col", swap))
        for apart in range(1, n_col // 2):
            g = gradient_of(2 * apart, g_wire, handed[apart - 1])
            back = [(i, (i - 2 * apart) % n_col) for i in range(n_col)]
            col_back.append(lax.ppermute(g, "col", back))
        col_back.append(lax.ppermute(gradient_of(1, g_wire), "col", swap))
    else:
        for stride in range(1, n_col):
            back = [(i, (i - stride) % n_col) for i in range(n_col)]
            g = gradient_of(stride, g_wire)
            col_back.append(lax.ppermute(g, "col", back))
    g_own = gradient_of(0, g_wide)

    (toward,) = call(
        functools.partial(toward_body, scale, cells),
        (jax.ShapeDtypeStruct((count, width), f32),),
        (*[weights[cell] for cell in range(cells)], *cell_rows),
        cells * dot_flops,
    )

    (base,) = call(gather_body, (g_wide,), (g_own, *col_back, *near_back[:-1]), 0)
    share = 1.0 / (count * n_row * n_col)
    loss, grad_passages = call(
        functools.partial(final_body, share, len(lost_parts)),
        (jax.ShapeDtypeStruct((1,), f32), g_wide),
        (base, near_back[-1], *lost_parts),
        0,
        out_specs=(pl.BlockSpec(memory_space=pltpu.SMEM), pl.BlockSpec(memory_space=pl.ANY)),
        scratch=(pltpu.VMEM((held, width), f32), pltpu.SemaphoreType.DMA((CHUNKS,))),
    )
    return (loss, toward, grad_passages)


def solution(mesh):
    return jax.shard_map(
        local_loss,
        mesh=mesh,
        in_specs=(
            P(("rep", "row", "col"), None),
            P(("rep", "row", "col"), None),
            P(("rep", "row", "col")),
            P(("rep", "row", "col"), None),
            P(("rep", "row", "col"), None),
        ),
        out_specs=(P("rep"), P(("rep", "row", "col"), None), P(("rep", "row", "col"), None)),
        check_vma=False,
    )
```

```python
import functools
import math

import jax
import jax.numpy as jnp
from jax import lax
from jax.experimental import pallas as pl
from jax.experimental.pallas import tpu as pltpu
from jax.sharding import PartitionSpec as P


BLK = 128
LOWEST = -1e30
LOG2E = math.log2(math.e)
VMEM_LIMIT = 24 << 20
CHUNKS = 4


def whole():
    return pl.BlockSpec(memory_space=pltpu.VMEM)


def call(kernel, outs, ins, flops, exps=0, out_specs=None, scratch=(), alias=None):
    moved = sum(a.size * a.dtype.itemsize for a in (*outs, *ins))
    return pl.pallas_call(
        kernel,
        out_shape=tuple(outs),
        in_specs=[
            pl.BlockSpec(memory_space=pl.ANY) if at == alias else whole() for at in range(len(ins))
        ],
        out_specs=out_specs or tuple(whole() for _ in outs),
        scratch_shapes=scratch,
        input_output_aliases={} if alias is None else {alias: len(outs) - 1},
        compiler_params=pltpu.CompilerParams(vmem_limit_bytes=VMEM_LIMIT),
        cost_estimate=pl.CostEstimate(flops=flops, bytes_accessed=moved, transcendentals=exps),
    )(*ins)


def block_stats(scores, block_at, scale):
    part = scores[block_at * BLK : (block_at + 1) * BLK]
    highest = jnp.max(part, axis=0, keepdims=True)
    raised = jnp.exp2((part - highest) * (scale * LOG2E))
    return part, highest, raised, jnp.sum(raised, axis=0, keepdims=True)


def scores_of(q_ref, p_ref):
    return lax.dot_general(
        p_ref[...], q_ref[...], (((1,), (1,)), ((), ())), preferred_element_type=jnp.float32
    )


def scores_body(scale, blocks, own, *refs):
    if own:
        q_ref, p_ref, pos_ref, e_ref, stats_ref = refs
    else:
        q_ref, p_ref, e_ref, stats_ref = refs
    scores = scores_of(q_ref, p_ref)
    stats_ref[...] = jnp.zeros_like(stats_ref)
    picked = None
    for block_at in range(blocks):
        part, highest, raised, summed = block_stats(scores, block_at, scale)
        e_ref[block_at * BLK : (block_at + 1) * BLK, :] = raised
        stats_ref[block_at : block_at + 1, :] = highest * scale
        stats_ref[blocks + block_at : blocks + block_at + 1, :] = summed
        if own:
            rows = lax.broadcasted_iota(jnp.int32, part.shape, 0) + block_at * BLK
            hit = jnp.sum(jnp.where(rows == pos_ref[...], part, 0.0), axis=0, keepdims=True)
            picked = hit if picked is None else picked + hit
    if own:
        stats_ref[2 * blocks : 2 * blocks + 1, :] = picked * scale


def weights_of(e_ref, f, blocks, pos):
    parts = []
    for block_at in range(blocks):
        part = e_ref[block_at * BLK : (block_at + 1) * BLK, :] * f[block_at : block_at + 1, :]
        if pos is not None:
            rows = lax.broadcasted_iota(jnp.int32, part.shape, 0) + block_at * BLK
            part = part - jnp.where(rows == pos, 1.0, 0.0)
        parts.append(part.astype(jnp.bfloat16))
    return jnp.concatenate(parts, axis=0)


def last_body(scale, blocks, cells, first, *refs):
    q_ref, p_ref, e_first_ref, vis_ref = refs[:4]
    stats_refs = refs[4 : 4 + cells - 1]
    e_ref, f_ref, head_ref, tail_ref, w_ref, loss_ref = refs[4 + cells - 1 :]
    scores = scores_of(q_ref, p_ref)
    tops, sums = [], []
    for block_at in range(blocks):
        _, highest, raised, summed = block_stats(scores, block_at, scale)
        e_ref[block_at * BLK : (block_at + 1) * BLK, :] = raised
        tops.append(highest * scale)
        sums.append(summed)
    all_tops = [s[0:blocks, :] for s in stats_refs] + [jnp.concatenate(tops, axis=0)]
    all_sums = [s[blocks : 2 * blocks, :] for s in stats_refs] + [jnp.concatenate(sums, axis=0)]
    seen = [vis_ref[cell * 8 : cell * 8 + blocks, :] > 0 for cell in range(cells)]
    highest = None
    for cell in range(cells):
        top = jnp.max(jnp.where(seen[cell], all_tops[cell], LOWEST), axis=0, keepdims=True)
        highest = top if highest is None else jnp.maximum(highest, top)
    total = None
    for cell in range(cells):
        gap = jnp.where(seen[cell], all_tops[cell] - highest, LOWEST)
        part = jnp.sum(all_sums[cell] * jnp.exp(gap), axis=0, keepdims=True)
        total = part if total is None else total + part
    log_total = highest + jnp.log(total)
    factors = []
    f_ref[...] = jnp.zeros_like(f_ref)
    for cell in range(cells):
        factor = jnp.exp(jnp.where(seen[cell], all_tops[cell] - log_total, LOWEST))
        f_ref[cell * 8 : cell * 8 + blocks, :] = factor
        factors.append(factor)
    positive_score = stats_refs[0][2 * blocks : 2 * blocks + 1, :]
    lost = jnp.sum(log_total - positive_score, axis=1, keepdims=True)
    loss_ref[...] = jnp.broadcast_to(lost, loss_ref.shape)
    weights = weights_of(e_first_ref, factors[first], blocks, None)
    w_ref[...] = weights
    put_pieces((head_ref, tail_ref), weights, q_ref, scale)


def put_pieces(pieces, weights, q_ref, scale):
    at = 0
    for ref in pieces:
        part = weights[at : at + ref.shape[0]]
        gradient = jnp.dot(part, q_ref[...], preferred_element_type=jnp.float32) * scale
        ref[...] = gradient.astype(ref.dtype)
        at += ref.shape[0]


def pieces_body(scale, blocks, cell, q_ref, e_ref, f_ref, head_ref, tail_ref, w_ref):
    weights = weights_of(e_ref, f_ref[cell * 8 : cell * 8 + 8, :], blocks, None)
    w_ref[...] = weights
    put_pieces((head_ref, tail_ref), weights, q_ref, scale)


def gradient_body(scale, blocks, cell, own, added, *refs):
    refs = list(refs)
    q_ref, e_ref, f_ref = refs[:3]
    del refs[:3]
    pos = refs.pop(0)[...] if own else None
    more_ref = refs.pop(0) if added else None
    g_ref, w_ref = refs
    weights = weights_of(e_ref, f_ref[cell * 8 : cell * 8 + 8, :], blocks, pos)
    w_ref[...] = weights
    gradient = jnp.dot(weights, q_ref[...], preferred_element_type=jnp.float32) * scale
    if added:
        gradient = gradient + more_ref[...].astype(jnp.float32)
    g_ref[...] = gradient.astype(g_ref.dtype)


def toward_body(scale, cells, *refs):
    w_refs, p_refs, out_ref = refs[:cells], refs[cells : 2 * cells], refs[2 * cells]
    total = None
    for w_ref, p_ref in zip(w_refs, p_refs):
        part = lax.dot_general(
            w_ref[...], p_ref[...], (((0,), (0,)), ((), ())), preferred_element_type=jnp.float32
        )
        total = part if total is None else total + part
    out_ref[...] = total * scale


def gather_body(wholes, *refs):
    out_ref, rest_ref, held_ref, sem = refs[-4:]
    heads = refs[wholes:-4]
    chunk = held_ref.shape[0] // CHUNKS
    copies = []
    for at in range(CHUNKS):
        rows = pl.ds(at * chunk, chunk)
        total = refs[0][rows, :]
        for ref in (*refs[1:wholes], *heads):
            total = total + ref[rows, :].astype(jnp.float32)
        held_ref[rows, :] = total
        copy = pltpu.make_async_copy(held_ref.at[rows, :], out_ref.at[rows, :], sem.at[at])
        copy.start()
        copies.append(copy)
    rows = pl.ds(held_ref.shape[0], rest_ref.shape[0])
    total = refs[0][rows, :]
    for ref in refs[1:wholes]:
        total = total + ref[rows, :].astype(jnp.float32)
    rest_ref[...] = total
    for copy in copies:
        copy.wait()


def final_body(share, tails, parts, rest_ref, *refs):
    tail_refs, lost_refs = refs[:tails], refs[tails : tails + parts]
    loss_ref, out_ref, held_ref, sem = refs[tails + parts + 1 :]
    first = out_ref.shape[0] - held_ref.shape[0]
    chunk = held_ref.shape[0] // CHUNKS
    copies = []
    for at in range(CHUNKS):
        rows = pl.ds(at * chunk, chunk)
        total = rest_ref[rows, :]
        for ref in tail_refs:
            total = total + ref[rows, :].astype(jnp.float32)
        held_ref[rows, :] = total
        there = out_ref.at[pl.ds(first + at * chunk, chunk), :]
        copy = pltpu.make_async_copy(held_ref.at[rows, :], there, sem.at[at])
        copy.start()
        copies.append(copy)
    total = lost_refs[0][...]
    for ref in lost_refs[1:]:
        total = total + ref[...]
    loss_ref[0] = jnp.max(total) * share
    for copy in copies:
        copy.wait()


def row_plan(n_row, reach):
    plan = []
    if reach == 1 and n_row % 2 == 0:
        even_up = [(i, i ^ 1) for i in range(n_row)]
        odd_up = [(i, (i + 1) % n_row if i % 2 else (i - 1) % n_row) for i in range(n_row)]
        plan.append((even_up, even_up, (2, 1)))
        plan.append((odd_up, odd_up, (1, 2)))
        return plan
    offsets = list(range(-reach, 0)) + list(range(1, reach + 1))
    for group_at, offset in enumerate(offsets):
        there = [((i + offset) % n_row, i) for i in range(n_row)]
        back = [(i, (i + offset) % n_row) for i in range(n_row)]
        plan.append((there, back, (group_at + 1, group_at + 1)))
    return plan


def sum_steps(array, axis):
    size = lax.axis_size(axis)
    if size & (size - 1):
        return lax.psum(array, axis)
    step = 1
    while step < size:
        pairs = [(i, i ^ step) for i in range(size)]
        array = array + lax.ppermute(array, axis, pairs)
        step *= 2
    return array


def from_all(array, axis):
    size = lax.axis_size(axis)
    if size > 4:
        return [sum_steps(array, axis)]
    shifts = range(1, size)
    return [array] + [
        lax.ppermute(array, axis, [(i, (i + s) % size) for i in range(size)]) for s in shifts
    ]


def local_loss(queries, passages, positive, block_mask, roster):
    n_row = lax.axis_size("row")
    n_col = lax.axis_size("col")
    reach = min(2, (n_row - 1) // 2)
    count, width = queries.shape
    held = passages.shape[0]
    blocks = held // BLK
    scale = width ** (-0.5)
    odd_row = lax.axis_index("row") % 2 == 1
    odd_col = lax.axis_index("col") % 2 == 1
    f32, bf16 = jnp.float32, jnp.bfloat16

    rows = row_plan(n_row, reach)
    near = [lax.ppermute(passages, "row", there) for there, _, _ in rows]

    swap = [(i, i ^ 1) for i in range(n_col)]
    col_cells = []
    paired = n_col % 2 == 0
    if paired:
        col_cells.append((lax.ppermute(passages, "col", swap), 1, n_col - 1))
        for apart in range(1, n_col // 2):
            there = [(i, (i + 2 * apart) % n_col) for i in range(n_col)]
            far = lax.ppermute(passages, "col", there)
            cross = lax.ppermute(far, "col", swap)
            col_cells.append((far, 2 * apart, 2 * apart))
            col_cells.append((cross, 2 * apart + 1, 2 * apart - 1))
    else:
        for stride in range(1, n_col):
            there = [(i, (i + stride) % n_col) for i in range(n_col)]
            far = lax.ppermute(passages, "col", there)
            col_cells.append((far, stride, stride))

    mask_t = block_mask.T
    roster_t = roster.T
    pos = positive.reshape(1, count)
    ids = jnp.arange(blocks, dtype=jnp.int32)[:, None]
    pad = jnp.zeros((8 - blocks, count), f32)

    def padded(flags):
        return jnp.concatenate([flags.astype(f32), pad], axis=0)

    def group_rows(group):
        return mask_t[group * blocks : (group + 1) * blocks] == 1

    seen = [padded(group_rows(0) | (pos // BLK == ids))]
    for _, odd, even in col_cells:
        seen.append(
            padded(jnp.where(odd_col, roster_t[odd - 1][None], roster_t[even - 1][None]) == ids)
        )
    for _, _, (even, odd) in rows:
        seen.append(padded(jnp.where(odd_row, group_rows(odd), group_rows(even))))
    vis = jnp.concatenate(seen, axis=0)

    cell_rows = [passages] + [cell[0] for cell in col_cells] + near
    cells = len(cell_rows)
    e_shape = jax.ShapeDtypeStruct((held, count), f32)
    w_shape = jax.ShapeDtypeStruct((held, count), bf16)
    s_shape = jax.ShapeDtypeStruct((8, count), f32)
    g_wire = jax.ShapeDtypeStruct((held, width), bf16)
    g_wide = jax.ShapeDtypeStruct((held, width), f32)
    dot_flops = 2 * held * count * width

    raised, stats = [], []
    for cell in range(cells - 1):
        own = cell == 0
        ins = (queries, cell_rows[cell]) + ((pos,) if own else ())
        e, s = call(
            functools.partial(scores_body, scale, blocks, own),
            (e_shape, s_shape),
            ins,
            dot_flops,
            held * count,
        )
        raised.append(e)
        stats.append(s)

    first = cells - len(rows)
    last = cells - 1
    f_shape = jax.ShapeDtypeStruct((8 * cells, count), f32)
    loss_shape = jax.ShapeDtypeStruct((8, BLK), f32)
    tail = BLK if blocks > 1 else 0
    assert tail
    head_shape = jax.ShapeDtypeStruct((held - tail, width), bf16)
    tail_shape = jax.ShapeDtypeStruct((tail, width), bf16)
    e, factors, g_head, g_tail, w_first, lost = call(
        functools.partial(last_body, scale, blocks, cells, first),
        (e_shape, f_shape, head_shape, tail_shape, w_shape, loss_shape),
        (queries, cell_rows[last], raised[first], vis, *stats),
        2 * dot_flops,
        held * count,
    )
    raised.append(e)
    weights = {first: w_first}

    def gradient_of(cell, shape, added=None):
        own = cell == 0
        ins = (queries, raised[cell], factors)
        ins += ((pos,) if own else ()) + (() if added is None else (added,))
        g, w = call(
            functools.partial(gradient_body, scale, blocks, cell, own, added is not None),
            (shape, w_shape),
            ins,
            dot_flops,
        )
        weights[cell] = w
        return g

    heads, tails = [(g_head, g_tail)], []
    for at in range(1, len(rows)):
        cell = first + at
        g_head, g_tail, weights[cell] = call(
            functools.partial(pieces_body, scale, blocks, cell),
            (head_shape, tail_shape, w_shape),
            (queries, raised[cell], factors),
            dot_flops,
        )
        heads.append((g_head, g_tail))
    for at, (_, back, _) in enumerate(rows):
        tails.append(lax.ppermute(heads[at][1], "row", back))
        heads[at] = lax.ppermute(heads[at][0], "row", back)

    lost_col = sum_steps(lost, "col")
    lost_parts = from_all(lost_col, "row")

    col_back = []
    if paired:
        handed = []
        for apart in range(1, n_col // 2):
            g = gradient_of(1 + 2 * apart, g_wire)
            handed.append(lax.ppermute(g, "col", swap))
        for apart in range(1, n_col // 2):
            g = gradient_of(2 * apart, g_wire, handed[apart - 1])
            back = [(i, (i - 2 * apart) % n_col) for i in range(n_col)]
            col_back.append(lax.ppermute(g, "col", back))
        col_back.append(lax.ppermute(gradient_of(1, g_wire), "col", swap))
    else:
        for stride in range(1, n_col):
            back = [(i, (i - stride) % n_col) for i in range(n_col)]
            g = gradient_of(stride, g_wire)
            col_back.append(lax.ppermute(g, "col", back))
    g_own = gradient_of(0, g_wide)

    (toward,) = call(
        functools.partial(toward_body, scale, cells),
        (jax.ShapeDtypeStruct((count, width), f32),),
        (*[weights[cell] for cell in range(cells)], *cell_rows),
        cells * dot_flops,
    )

    wides = (g_own, *col_back)
    wire_sems = pltpu.SemaphoreType.DMA((CHUNKS,))
    rest_shape = jax.ShapeDtypeStruct((tail, width), f32)
    out_spec = pl.BlockSpec(memory_space=pl.ANY)
    written, rest = call(
        functools.partial(gather_body, len(wides)),
        (g_wide, rest_shape),
        (*wides, *heads),
        0,
        out_specs=(out_spec, whole()),
        scratch=(pltpu.VMEM((held - tail, width), f32), wire_sems),
    )
    share = 1.0 / (count * n_row * n_col)
    loss, grad_passages = call(
        functools.partial(final_body, share, len(tails), len(lost_parts)),
        (jax.ShapeDtypeStruct((1,), f32), g_wide),
        (rest, *tails, *lost_parts, written),
        0,
        out_specs=(pl.BlockSpec(memory_space=pltpu.SMEM), out_spec),
        scratch=(pltpu.VMEM((tail, width), f32), wire_sems),
        alias=1 + len(tails) + len(lost_parts),
    )
    return (loss, toward, grad_passages)


def solution(mesh):
    return jax.shard_map(
        local_loss,
        mesh=mesh,
        in_specs=(
            P(("rep", "row", "col"), None),
            P(("rep", "row", "col"), None),
            P(("rep", "row", "col")),
            P(("rep", "row", "col"), None),
            P(("rep", "row", "col"), None),
        ),
        out_specs=(P("rep"), P(("rep", "row", "col"), None), P(("rep", "row", "col"), None)),
        check_vma=False,
    )
```

```python
import functools
import math

import jax
import jax.numpy as jnp
from jax import lax
from jax.experimental import pallas as pl
from jax.experimental.pallas import tpu as pltpu
from jax.sharding import PartitionSpec as P


BLK = 128
LOWEST = -1e30
LOG2E = math.log2(math.e)
VMEM_LIMIT = 24 << 20
CHUNKS = 2


def whole():
    return pl.BlockSpec(memory_space=pltpu.VMEM)


def call(kernel, outs, ins, flops, exps=0, out_specs=None, scratch=(), alias=None):
    moved = sum(a.size * a.dtype.itemsize for a in (*outs, *ins))
    return pl.pallas_call(
        kernel,
        out_shape=tuple(outs),
        in_specs=[
            pl.BlockSpec(memory_space=pl.ANY) if at == alias else whole() for at in range(len(ins))
        ],
        out_specs=out_specs or tuple(whole() for _ in outs),
        scratch_shapes=scratch,
        input_output_aliases={} if alias is None else {alias: len(outs) - 1},
        compiler_params=pltpu.CompilerParams(vmem_limit_bytes=VMEM_LIMIT),
        cost_estimate=pl.CostEstimate(flops=flops, bytes_accessed=moved, transcendentals=exps),
    )(*ins)


def block_stats(scores, block_at, scale):
    part = scores[block_at * BLK : (block_at + 1) * BLK]
    highest = jnp.max(part, axis=0, keepdims=True)
    raised = jnp.exp2((part - highest) * (scale * LOG2E))
    return part, highest, raised, jnp.sum(raised, axis=0, keepdims=True)


def scores_of(q_ref, p_ref):
    return lax.dot_general(
        p_ref[...], q_ref[...], (((1,), (1,)), ((), ())), preferred_element_type=jnp.float32
    )


def scores_body(scale, blocks, own, *refs):
    if own:
        q_ref, p_ref, pos_ref, e_ref, stats_ref = refs
    else:
        q_ref, p_ref, e_ref, stats_ref = refs
    scores = scores_of(q_ref, p_ref)
    stats_ref[...] = jnp.zeros_like(stats_ref)
    picked = None
    for block_at in range(blocks):
        part, highest, raised, summed = block_stats(scores, block_at, scale)
        e_ref[block_at * BLK : (block_at + 1) * BLK, :] = raised
        stats_ref[block_at : block_at + 1, :] = highest * scale
        stats_ref[blocks + block_at : blocks + block_at + 1, :] = summed
        if own:
            rows = lax.broadcasted_iota(jnp.int32, part.shape, 0) + block_at * BLK
            hit = jnp.sum(jnp.where(rows == pos_ref[...], part, 0.0), axis=0, keepdims=True)
            picked = hit if picked is None else picked + hit
    if own:
        stats_ref[2 * blocks : 2 * blocks + 1, :] = picked * scale


def weights_of(e_ref, f, blocks, pos):
    parts = []
    for block_at in range(blocks):
        part = e_ref[block_at * BLK : (block_at + 1) * BLK, :] * f[block_at : block_at + 1, :]
        if pos is not None:
            rows = lax.broadcasted_iota(jnp.int32, part.shape, 0) + block_at * BLK
            part = part - jnp.where(rows == pos, 1.0, 0.0)
        parts.append(part.astype(jnp.bfloat16))
    return jnp.concatenate(parts, axis=0)


def last_body(scale, blocks, cells, *refs):
    q_ref, p_ref, vis_ref = refs[:3]
    stats_refs = refs[3 : 3 + cells - 1]
    f_ref, head_ref, tail_ref, w_ref, loss_ref, e_ref = refs[3 + cells - 1 :]
    scores = scores_of(q_ref, p_ref)
    tops, sums = [], []
    for block_at in range(blocks):
        _, highest, raised, summed = block_stats(scores, block_at, scale)
        e_ref[block_at * BLK : (block_at + 1) * BLK, :] = raised
        tops.append(highest * scale)
        sums.append(summed)
    all_tops = [s[0:blocks, :] for s in stats_refs] + [jnp.concatenate(tops, axis=0)]
    all_sums = [s[blocks : 2 * blocks, :] for s in stats_refs] + [jnp.concatenate(sums, axis=0)]
    seen = [vis_ref[cell * 8 : cell * 8 + blocks, :] > 0 for cell in range(cells)]
    highest = None
    for cell in range(cells):
        top = jnp.max(jnp.where(seen[cell], all_tops[cell], LOWEST), axis=0, keepdims=True)
        highest = top if highest is None else jnp.maximum(highest, top)
    total = None
    for cell in range(cells):
        gap = jnp.where(seen[cell], all_tops[cell] - highest, LOWEST)
        part = jnp.sum(all_sums[cell] * jnp.exp(gap), axis=0, keepdims=True)
        total = part if total is None else total + part
    log_total = highest + jnp.log(total)
    f_ref[...] = jnp.zeros_like(f_ref)
    for cell in range(cells):
        factor = jnp.exp(jnp.where(seen[cell], all_tops[cell] - log_total, LOWEST))
        f_ref[cell * 8 : cell * 8 + blocks, :] = factor
    positive_score = stats_refs[0][2 * blocks : 2 * blocks + 1, :]
    lost = jnp.sum(log_total - positive_score, axis=1, keepdims=True)
    loss_ref[...] = jnp.broadcast_to(lost, loss_ref.shape)
    weights = weights_of(e_ref, factor, blocks, None)
    w_ref[...] = weights
    put_pieces((head_ref, tail_ref), weights, q_ref, scale)


def put_pieces(pieces, weights, q_ref, scale):
    at = 0
    for ref in pieces:
        part = weights[at : at + ref.shape[0]]
        gradient = jnp.dot(part, q_ref[...], preferred_element_type=jnp.float32) * scale
        ref[...] = gradient.astype(ref.dtype)
        at += ref.shape[0]


def pieces_body(scale, blocks, cell, q_ref, e_ref, f_ref, head_ref, tail_ref, w_ref):
    weights = weights_of(e_ref, f_ref[cell * 8 : cell * 8 + 8, :], blocks, None)
    w_ref[...] = weights
    put_pieces((head_ref, tail_ref), weights, q_ref, scale)


def gradient_body(scale, blocks, cell, own, added, *refs):
    refs = list(refs)
    q_ref, e_ref, f_ref = refs[:3]
    del refs[:3]
    pos = refs.pop(0)[...] if own else None
    more_ref = refs.pop(0) if added else None
    g_ref, w_ref = refs
    weights = weights_of(e_ref, f_ref[cell * 8 : cell * 8 + 8, :], blocks, pos)
    w_ref[...] = weights
    gradient = jnp.dot(weights, q_ref[...], preferred_element_type=jnp.float32) * scale
    if added:
        gradient = gradient + more_ref[...].astype(jnp.float32)
    g_ref[...] = gradient.astype(g_ref.dtype)


def toward_body(scale, cells, *refs):
    w_refs, p_refs, out_ref = refs[:cells], refs[cells : 2 * cells], refs[2 * cells]
    total = None
    for w_ref, p_ref in zip(w_refs, p_refs):
        part = lax.dot_general(
            w_ref[...], p_ref[...], (((0,), (0,)), ((), ())), preferred_element_type=jnp.float32
        )
        total = part if total is None else total + part
    out_ref[...] = total * scale


def gather_body(wholes, *refs):
    out_ref, rest_ref, held_ref, sem = refs[-4:]
    heads = refs[wholes:-4]
    chunk = held_ref.shape[0] // CHUNKS
    copies = []
    for at in range(CHUNKS):
        rows = pl.ds(at * chunk, chunk)
        total = refs[0][rows, :]
        for ref in (*refs[1:wholes], *heads):
            total = total + ref[rows, :].astype(jnp.float32)
        held_ref[rows, :] = total
        copy = pltpu.make_async_copy(held_ref.at[rows, :], out_ref.at[rows, :], sem.at[at])
        copy.start()
        copies.append(copy)
    rows = pl.ds(held_ref.shape[0], rest_ref.shape[0])
    total = refs[0][rows, :]
    for ref in refs[1:wholes]:
        total = total + ref[rows, :].astype(jnp.float32)
    rest_ref[...] = total
    for copy in copies:
        copy.wait()


def final_body(share, tails, parts, rest_ref, *refs):
    tail_refs, lost_refs = refs[:tails], refs[tails : tails + parts]
    loss_ref, out_ref, held_ref, sem, loss_sm, loss_sem = refs[tails + parts + 1 :]
    total = lost_refs[0][...]
    for ref in lost_refs[1:]:
        total = total + ref[...]
    loss_sm[0] = jnp.max(total) * share
    copies = [pltpu.make_async_copy(loss_sm, loss_ref, loss_sem)]
    copies[0].start()
    first = out_ref.shape[0] - held_ref.shape[0]
    chunk = held_ref.shape[0] // CHUNKS
    for at in range(CHUNKS):
        rows = pl.ds(at * chunk, chunk)
        total = rest_ref[rows, :]
        for ref in tail_refs:
            total = total + ref[rows, :].astype(jnp.float32)
        held_ref[rows, :] = total
        there = out_ref.at[pl.ds(first + at * chunk, chunk), :]
        copy = pltpu.make_async_copy(held_ref.at[rows, :], there, sem.at[at])
        copy.start()
        copies.append(copy)
    for copy in copies:
        copy.wait()


def row_plan(n_row, n_col, reach):
    cells = [(r, c) for r in range(n_row) for c in range(n_col)]

    def pairs(partner):
        return [(r * n_col + c, partner(r, c) % n_row * n_col + c) for r, c in cells]

    if reach == 1 and n_row % 2 == 0:
        first = pairs(lambda r, c: r + 1 if (r + c) % 2 == 0 else r - 1)
        second = pairs(lambda r, c: r - 1 if (r + c) % 2 == 0 else r + 1)
        return [(first, first, (2, 1)), (second, second, (1, 2))]
    plan = []
    offsets = list(range(-reach, 0)) + list(range(1, reach + 1))
    for group_at, offset in enumerate(offsets):
        there = pairs(lambda r, c: r - offset)
        back = pairs(lambda r, c: r + offset)
        plan.append((there, back, (group_at + 1, group_at + 1)))
    return plan


def sum_steps(array, axis):
    size = lax.axis_size(axis)
    if size & (size - 1):
        return lax.psum(array, axis)
    step = 1
    while step < size:
        pairs = [(i, i ^ step) for i in range(size)]
        array = array + lax.ppermute(array, axis, pairs)
        step *= 2
    return array


def partners(size, step):
    if size & (size - 1):
        return [(i, (i + step) % size) for i in range(size)]
    return [(i, i ^ step) for i in range(size)]


def from_all(array, axis):
    size = lax.axis_size(axis)
    if size > 4:
        return [sum_steps(array, axis)]
    shifts = range(1, size)
    return [array] + [lax.ppermute(array, axis, partners(size, s)) for s in shifts]


def local_loss(queries, passages, positive, block_mask, roster):
    n_row = lax.axis_size("row")
    n_col = lax.axis_size("col")
    reach = min(2, (n_row - 1) // 2)
    count, width = queries.shape
    held = passages.shape[0]
    blocks = held // BLK
    scale = width ** (-0.5)
    odd_col = lax.axis_index("col") % 2 == 1
    odd_cell = (lax.axis_index("row") + lax.axis_index("col")) % 2 == 1
    f32, bf16 = jnp.float32, jnp.bfloat16

    rows = row_plan(n_row, n_col, reach)
    near = [lax.ppermute(passages, ("row", "col"), there) for there, _, _ in rows]

    swap = [(i, i ^ 1) for i in range(n_col)]
    col_cells = []
    paired = n_col % 2 == 0
    if paired:
        col_cells.append((lax.ppermute(passages, "col", swap), 1, n_col - 1))
        for apart in range(1, n_col // 2):
            there = [(i, (i + 2 * apart) % n_col) for i in range(n_col)]
            far = lax.ppermute(passages, "col", there)
            cross = lax.ppermute(far, "col", swap)
            col_cells.append((far, 2 * apart, 2 * apart))
            col_cells.append((cross, 2 * apart + 1, 2 * apart - 1))
    else:
        for stride in range(1, n_col):
            there = [(i, (i + stride) % n_col) for i in range(n_col)]
            far = lax.ppermute(passages, "col", there)
            col_cells.append((far, stride, stride))

    mask_t = block_mask.T
    roster_t = roster.T
    pos = positive.reshape(1, count)
    ids = jnp.arange(blocks, dtype=jnp.int32)[:, None]
    pad = jnp.zeros((8 - blocks, count), f32)

    def padded(flags):
        return jnp.concatenate([flags.astype(f32), pad], axis=0)

    def group_rows(group):
        return mask_t[group * blocks : (group + 1) * blocks] == 1

    seen = [padded(group_rows(0) | (pos // BLK == ids))]
    for _, odd, even in col_cells:
        seen.append(
            padded(jnp.where(odd_col, roster_t[odd - 1][None], roster_t[even - 1][None]) == ids)
        )
    for _, _, (even, odd) in rows:
        seen.append(padded(jnp.where(odd_cell, group_rows(odd), group_rows(even))))
    vis = jnp.concatenate(seen, axis=0)

    cell_rows = [passages] + [cell[0] for cell in col_cells] + near
    cells = len(cell_rows)
    e_shape = jax.ShapeDtypeStruct((held, count), f32)
    w_shape = jax.ShapeDtypeStruct((held, count), bf16)
    s_shape = jax.ShapeDtypeStruct((8, count), f32)
    g_wire = jax.ShapeDtypeStruct((held, width), bf16)
    g_wide = jax.ShapeDtypeStruct((held, width), f32)
    dot_flops = 2 * held * count * width

    raised, stats = [], []
    for cell in range(cells - 1):
        own = cell == 0
        ins = (queries, cell_rows[cell]) + ((pos,) if own else ())
        e, s = call(
            functools.partial(scores_body, scale, blocks, own),
            (e_shape, s_shape),
            ins,
            dot_flops,
            held * count,
        )
        raised.append(e)
        stats.append(s)

    first = cells - len(rows)
    last = cells - 1
    f_shape = jax.ShapeDtypeStruct((8 * cells, count), f32)
    loss_shape = jax.ShapeDtypeStruct((8, BLK), f32)
    tail = BLK
    head_shape = jax.ShapeDtypeStruct((held - tail, width), bf16)
    tail_shape = jax.ShapeDtypeStruct((tail, width), bf16)
    factors, g_head, g_tail, w_last, lost = call(
        functools.partial(last_body, scale, blocks, cells),
        (f_shape, head_shape, tail_shape, w_shape, loss_shape),
        (queries, cell_rows[last], vis, *stats),
        2 * dot_flops,
        held * count,
        scratch=(pltpu.VMEM((held, count), f32),),
    )
    weights = {last: w_last}

    def gradient_of(cell, shape, added=None):
        own = cell == 0
        ins = (queries, raised[cell], factors)
        ins += ((pos,) if own else ()) + (() if added is None else (added,))
        g, w = call(
            functools.partial(gradient_body, scale, blocks, cell, own, added is not None),
            (shape, w_shape),
            ins,
            dot_flops,
        )
        weights[cell] = w
        return g

    graded = {len(rows) - 1: (g_head, g_tail)}
    for at in range(len(rows) - 1):
        cell = first + at
        g_head, g_tail, weights[cell] = call(
            functools.partial(pieces_body, scale, blocks, cell),
            (head_shape, tail_shape, w_shape),
            (queries, raised[cell], factors),
            dot_flops,
        )
        graded[at] = (g_head, g_tail)
    heads, tails = [], []
    for at, (_, back, _) in enumerate(rows):
        heads.append(lax.ppermute(graded[at][0], ("row", "col"), back))
        tails.append(lax.ppermute(graded[at][1], ("row", "col"), back))

    lost_col = sum_steps(lost, "col")
    lost_parts = from_all(lost_col, "row")

    col_back = []
    if paired:
        handed = []
        for apart in range(1, n_col // 2):
            g = gradient_of(1 + 2 * apart, g_wire)
            handed.append(lax.ppermute(g, "col", swap))
        for apart in range(1, n_col // 2):
            g = gradient_of(2 * apart, g_wire, handed[apart - 1])
            back = [(i, (i - 2 * apart) % n_col) for i in range(n_col)]
            col_back.append(lax.ppermute(g, "col", back))
        col_back.append(lax.ppermute(gradient_of(1, g_wire), "col", swap))
    else:
        for stride in range(1, n_col):
            back = [(i, (i - stride) % n_col) for i in range(n_col)]
            g = gradient_of(stride, g_wire)
            col_back.append(lax.ppermute(g, "col", back))
    g_own = gradient_of(0, g_wide)

    (toward,) = call(
        functools.partial(toward_body, scale, cells),
        (jax.ShapeDtypeStruct((count, width), f32),),
        (*[weights[cell] for cell in range(cells)], *cell_rows),
        cells * dot_flops,
    )

    wides = (g_own, *col_back)
    wire_sems = pltpu.SemaphoreType.DMA((CHUNKS,))
    rest_shape = jax.ShapeDtypeStruct((tail, width), f32)
    out_spec = pl.BlockSpec(memory_space=pl.ANY)
    written, rest = call(
        functools.partial(gather_body, len(wides)),
        (g_wide, rest_shape),
        (*wides, *heads),
        0,
        out_specs=(out_spec, whole()),
        scratch=(pltpu.VMEM((held - tail, width), f32), wire_sems),
    )
    share = 1.0 / (count * n_row * n_col)
    loss, grad_passages = call(
        functools.partial(final_body, share, len(tails), len(lost_parts)),
        (jax.ShapeDtypeStruct((1,), f32), g_wide),
        (rest, *tails, *lost_parts, written),
        0,
        out_specs=(out_spec, out_spec),
        scratch=(pltpu.VMEM((tail, width), f32), wire_sems, pltpu.SMEM((1,), f32), pltpu.SemaphoreType.DMA),
        alias=1 + len(tails) + len(lost_parts),
    )
    return (loss, toward, grad_passages)


def solution(mesh):
    return jax.shard_map(
        local_loss,
        mesh=mesh,
        in_specs=(
            P(("rep", "row", "col"), None),
            P(("rep", "row", "col"), None),
            P(("rep", "row", "col")),
            P(("rep", "row", "col"), None),
            P(("rep", "row", "col"), None),
        ),
        out_specs=(P("rep"), P(("rep", "row", "col"), None), P(("rep", "row", "col"), None)),
        check_vma=False,
    )
```

```python
import functools
import math

import jax
import jax.numpy as jnp
from jax import lax
from jax.experimental import pallas as pl
from jax.experimental.pallas import tpu as pltpu
from jax.sharding import PartitionSpec as P


BLK = 128
LOWEST = -1e30
LOG2E = math.log2(math.e)
VMEM_LIMIT = 24 << 20
CHUNKS = 2


def whole():
    return pl.BlockSpec(memory_space=pltpu.VMEM)


def call(kernel, outs, ins, flops, exps=0, out_specs=None, scratch=(), alias=None):
    moved = sum(a.size * a.dtype.itemsize for a in (*outs, *ins))
    return pl.pallas_call(
        kernel,
        out_shape=tuple(outs),
        in_specs=[
            pl.BlockSpec(memory_space=pl.ANY) if at == alias else whole() for at in range(len(ins))
        ],
        out_specs=out_specs or tuple(whole() for _ in outs),
        scratch_shapes=scratch,
        input_output_aliases={} if alias is None else {alias: len(outs) - 1},
        compiler_params=pltpu.CompilerParams(vmem_limit_bytes=VMEM_LIMIT),
        cost_estimate=pl.CostEstimate(flops=flops, bytes_accessed=moved, transcendentals=exps),
    )(*ins)


def block_stats(scores, block_at, scale):
    part = scores[block_at * BLK : (block_at + 1) * BLK]
    highest = jnp.max(part, axis=0, keepdims=True)
    raised = jnp.exp2((part - highest) * (scale * LOG2E))
    return part, highest, raised, jnp.sum(raised, axis=0, keepdims=True)


def scores_of(q_ref, p_ref):
    return lax.dot_general(
        p_ref[...], q_ref[...], (((1,), (1,)), ((), ())), preferred_element_type=jnp.float32
    )


def vis_body(blocks, col_strides, row_groups, mask_ref, roster_ref, pos_ref, out_ref):
    odd_row = (lax.axis_index("row") + lax.axis_index("col")) % 2
    odd_col = lax.axis_index("col") % 2
    height = out_ref.shape[0]
    strides = [jnp.where(odd_col == 1, odd, even) - 1 for odd, even in col_strides]
    groups = [jnp.where(odd_row == 1, odd, even) for even, odd in row_groups]
    first_row = 1 + len(strides)

    def chosen(flags_ref, columns):
        shape = (height, flags_ref.shape[0])
        cell = lax.broadcasted_iota(jnp.int32, shape, 0) // 8
        block = lax.broadcasted_iota(jnp.int32, shape, 0) % 8
        wanted = jnp.full(shape, -1, jnp.int32)
        for at, column, step in columns:
            wanted = jnp.where(cell == at, column + step * block, wanted)
        picks = lax.broadcasted_iota(jnp.int32, shape, 1) == wanted
        picks = jnp.where(picks & (block < blocks), 1.0, 0.0)
        return lax.dot_general(
            picks,
            flags_ref[...].astype(jnp.float32),
            (((1,), (0,)), ((), ())),
            preferred_element_type=jnp.float32,
        )

    masked = [(0, 0, 1)]
    masked += [(first_row + at, group * blocks, 1) for at, group in enumerate(groups)]
    seen = chosen(mask_ref, masked)
    drawn = chosen(roster_ref, [(1 + at, stride, 0) for at, stride in enumerate(strides)])
    cell = lax.broadcasted_iota(jnp.int32, seen.shape, 0) // 8
    block = lax.broadcasted_iota(jnp.int32, seen.shape, 0) % 8
    inside = block < blocks
    column = (cell >= 1) & (cell < first_row)
    held = (cell == 0) & (pos_ref[...] // BLK == block)
    visited = column & (drawn.astype(jnp.int32) == block)
    out_ref[...] = jnp.where(inside & (held | visited | (seen > 0.5)), 1.0, 0.0)


def scores_body(scale, blocks, own, *refs):
    q_ref, p_ref, pos_ref = refs[0], refs[1], refs[2]
    e_ref, stats_ref = refs[-2:]
    scores = scores_of(q_ref, p_ref)
    stats_ref[...] = jnp.zeros_like(stats_ref)
    picked = None
    for block_at in range(blocks):
        part, highest, raised, summed = block_stats(scores, block_at, scale)
        e_ref[block_at * BLK : (block_at + 1) * BLK, :] = raised
        stats_ref[block_at : block_at + 1, :] = highest * scale
        stats_ref[blocks + block_at : blocks + block_at + 1, :] = summed
        if own:
            rows = lax.broadcasted_iota(jnp.int32, part.shape, 0) + block_at * BLK
            hit = jnp.sum(jnp.where(rows == pos_ref[...], part, 0.0), axis=0, keepdims=True)
            picked = hit if picked is None else picked + hit
    if own:
        stats_ref[2 * blocks : 2 * blocks + 1, :] = picked * scale


def weights_of(e_ref, f, blocks, pos):
    parts = []
    for block_at in range(blocks):
        part = e_ref[block_at * BLK : (block_at + 1) * BLK, :] * f[block_at : block_at + 1, :]
        if pos is not None:
            rows = lax.broadcasted_iota(jnp.int32, part.shape, 0) + block_at * BLK
            part = part - jnp.where(rows == pos, 1.0, 0.0)
        parts.append(part.astype(jnp.bfloat16))
    return jnp.concatenate(parts, axis=0)


def last_body(scale, blocks, cells, *refs):
    f_ref, head_ref, w_ref, loss_ref, e_ref = refs[-5:]
    q_ref, p_ref, vis_ref = refs[:3]
    stats_refs = refs[3:-5]
    scores = scores_of(q_ref, p_ref)
    tops, sums = [], []
    for block_at in range(blocks):
        _, highest, raised, summed = block_stats(scores, block_at, scale)
        e_ref[block_at * BLK : (block_at + 1) * BLK, :] = raised
        tops.append(highest * scale)
        sums.append(summed)
    all_tops = [s[0:blocks, :] for s in stats_refs] + [jnp.concatenate(tops, axis=0)]
    all_sums = [s[blocks : 2 * blocks, :] for s in stats_refs] + [jnp.concatenate(sums, axis=0)]
    seen = [vis_ref[cell * 8 : cell * 8 + blocks, :] > 0 for cell in range(cells)]
    highest = None
    for cell in range(cells):
        top = jnp.max(jnp.where(seen[cell], all_tops[cell], LOWEST), axis=0, keepdims=True)
        highest = top if highest is None else jnp.maximum(highest, top)
    total = None
    for cell in range(cells):
        gap = jnp.where(seen[cell], all_tops[cell] - highest, LOWEST)
        part = jnp.sum(all_sums[cell] * jnp.exp(gap), axis=0, keepdims=True)
        total = part if total is None else total + part
    log_total = highest + jnp.log(total)
    f_ref[...] = jnp.zeros_like(f_ref)
    for cell in range(cells):
        factor = jnp.exp(jnp.where(seen[cell], all_tops[cell] - log_total, LOWEST))
        f_ref[cell * 8 : cell * 8 + blocks, :] = factor
    positive_score = stats_refs[0][2 * blocks : 2 * blocks + 1, :]
    lost = jnp.sum(log_total - positive_score, axis=1, keepdims=True)
    loss_ref[...] = jnp.broadcast_to(lost, loss_ref.shape)
    weights = weights_of(e_ref, factor, blocks, None)
    w_ref[...] = weights
    put_pieces((head_ref,), weights, q_ref, scale)


def put_pieces(pieces, weights, q_ref, scale):
    at = 0
    for ref in pieces:
        part = weights[at : at + ref.shape[0]]
        gradient = jnp.dot(part, q_ref[...], preferred_element_type=jnp.float32) * scale
        ref[...] = gradient.astype(ref.dtype)
        at += ref.shape[0]


def tail_body(scale, q_ref, w_ref, tail_ref):
    part = w_ref[w_ref.shape[0] - tail_ref.shape[0] :, :]
    gradient = jnp.dot(part, q_ref[...], preferred_element_type=jnp.float32) * scale
    tail_ref[...] = gradient.astype(tail_ref.dtype)


def pieces_body(scale, blocks, cell, q_ref, e_ref, f_ref, head_ref, tail_ref, w_ref):
    weights = weights_of(e_ref, f_ref[cell * 8 : cell * 8 + 8, :], blocks, None)
    w_ref[...] = weights
    put_pieces((head_ref, tail_ref), weights, q_ref, scale)


def gradient_body(scale, blocks, cell, own, added, *refs):
    refs = list(refs)
    q_ref, e_ref, f_ref = refs[:3]
    del refs[:3]
    pos = refs.pop(0)[...] if own else None
    more_ref = refs.pop(0) if added else None
    g_ref, w_ref = refs
    weights = weights_of(e_ref, f_ref[cell * 8 : cell * 8 + 8, :], blocks, pos)
    w_ref[...] = weights
    gradient = jnp.dot(weights, q_ref[...], preferred_element_type=jnp.float32) * scale
    if added:
        gradient = gradient + more_ref[...].astype(jnp.float32)
    g_ref[...] = gradient.astype(g_ref.dtype)


def toward_body(scale, cells, *refs):
    w_refs, p_refs, out_ref = refs[:cells], refs[cells : 2 * cells], refs[2 * cells]
    total = None
    for w_ref, p_ref in zip(w_refs, p_refs):
        part = lax.dot_general(
            w_ref[...], p_ref[...], (((0,), (0,)), ((), ())), preferred_element_type=jnp.float32
        )
        total = part if total is None else total + part
    out_ref[...] = total * scale


def gather_body(wholes, *refs):
    out_ref, rest_ref, held_ref, sem = refs[-4:]
    heads = refs[wholes:-4]
    chunk = held_ref.shape[0] // CHUNKS
    copies = []
    for at in range(CHUNKS):
        rows = pl.ds(at * chunk, chunk)
        total = refs[0][rows, :]
        for ref in (*refs[1:wholes], *heads):
            total = total + ref[rows, :].astype(jnp.float32)
        held_ref[rows, :] = total
        copy = pltpu.make_async_copy(held_ref.at[rows, :], out_ref.at[rows, :], sem.at[at])
        copy.start()
        copies.append(copy)
    rows = pl.ds(held_ref.shape[0], rest_ref.shape[0])
    total = refs[0][rows, :]
    for ref in refs[1:wholes]:
        total = total + ref[rows, :].astype(jnp.float32)
    rest_ref[...] = total
    for copy in copies:
        copy.wait()


def final_body(share, tails, parts, rest_ref, *refs):
    tail_refs, lost_refs = refs[:tails], refs[tails : tails + parts]
    loss_ref, out_ref, held_ref, sem, loss_sm, loss_sem = refs[tails + parts + 1 :]
    total = lost_refs[0][...]
    for ref in lost_refs[1:]:
        total = total + ref[...]
    loss_sm[0] = jnp.max(total) * share
    copies = [pltpu.make_async_copy(loss_sm, loss_ref, loss_sem)]
    copies[0].start()
    first = out_ref.shape[0] - held_ref.shape[0]
    chunk = held_ref.shape[0] // CHUNKS
    for at in range(CHUNKS):
        rows = pl.ds(at * chunk, chunk)
        total = rest_ref[rows, :]
        for ref in tail_refs:
            total = total + ref[rows, :].astype(jnp.float32)
        held_ref[rows, :] = total
        there = out_ref.at[pl.ds(first + at * chunk, chunk), :]
        copy = pltpu.make_async_copy(held_ref.at[rows, :], there, sem.at[at])
        copy.start()
        copies.append(copy)
    for copy in copies:
        copy.wait()


def row_plan(n_row, n_col, reach):
    cells = [(r, c) for r in range(n_row) for c in range(n_col)]

    def pairs(partner):
        return [(r * n_col + c, partner(r, c) % n_row * n_col + c) for r, c in cells]

    if reach == 1 and n_row % 2 == 0:
        first = pairs(lambda r, c: r + 1 if (r + c) % 2 == 0 else r - 1)
        second = pairs(lambda r, c: r - 1 if (r + c) % 2 == 0 else r + 1)
        return [(first, first, (2, 1)), (second, second, (1, 2))]
    plan = []
    offsets = list(range(-reach, 0)) + list(range(1, reach + 1))
    for group_at, offset in enumerate(offsets):
        there = pairs(lambda r, c: r - offset)
        back = pairs(lambda r, c: r + offset)
        plan.append((there, back, (group_at + 1, group_at + 1)))
    return plan


def sum_steps(array, axis):
    size = lax.axis_size(axis)
    if size & (size - 1):
        return lax.psum(array, axis)
    step = 1
    while step < size:
        pairs = [(i, i ^ step) for i in range(size)]
        array = array + lax.ppermute(array, axis, pairs)
        step *= 2
    return array


def partners(size, step):
    if size & (size - 1):
        return [(i, (i + step) % size) for i in range(size)]
    return [(i, i ^ step) for i in range(size)]


def from_all(array, axis):
    size = lax.axis_size(axis)
    if size > 4:
        return [sum_steps(array, axis)]
    shifts = range(1, size)
    return [array] + [lax.ppermute(array, axis, partners(size, s)) for s in shifts]


def local_loss(queries, passages, positive, block_mask, roster):
    n_row = lax.axis_size("row")
    n_col = lax.axis_size("col")
    reach = min(2, (n_row - 1) // 2)
    count, width = queries.shape
    held = passages.shape[0]
    blocks = held // BLK
    scale = width ** (-0.5)
    f32, bf16 = jnp.float32, jnp.bfloat16

    rows = row_plan(n_row, n_col, reach)
    near = [lax.ppermute(passages, ("row", "col"), there) for there, _, _ in rows]

    swap = [(i, i ^ 1) for i in range(n_col)]
    col_cells = []
    paired = n_col % 2 == 0
    if paired:
        col_cells.append((lax.ppermute(passages, "col", swap), 1, n_col - 1))
        for apart in range(1, n_col // 2):
            there = [(i, (i + 2 * apart) % n_col) for i in range(n_col)]
            far = lax.ppermute(passages, "col", there)
            cross = lax.ppermute(far, "col", swap)
            col_cells.append((far, 2 * apart, 2 * apart))
            col_cells.append((cross, 2 * apart + 1, 2 * apart - 1))
    else:
        for stride in range(1, n_col):
            there = [(i, (i + stride) % n_col) for i in range(n_col)]
            far = lax.ppermute(passages, "col", there)
            col_cells.append((far, stride, stride))

    pos = positive.reshape(1, count)
    (vis,) = call(
        functools.partial(
            vis_body,
            blocks,
            [(odd, even) for _, odd, even in col_cells],
            [groups for _, _, groups in rows],
        ),
        (jax.ShapeDtypeStruct((8 * (1 + len(col_cells) + len(rows)), count), f32),),
        (block_mask.T, roster.T, pos),
        0,
    )

    cell_rows = [passages] + [cell[0] for cell in col_cells] + near
    cells = len(cell_rows)
    e_shape = jax.ShapeDtypeStruct((held, count), f32)
    w_shape = jax.ShapeDtypeStruct((held, count), bf16)
    s_shape = jax.ShapeDtypeStruct((8, count), f32)
    g_wire = jax.ShapeDtypeStruct((held, width), bf16)
    g_wide = jax.ShapeDtypeStruct((held, width), f32)
    dot_flops = 2 * held * count * width

    raised, stats = [], []
    for cell in range(cells - 1):
        own = cell == 0
        ins = (queries, cell_rows[cell]) + ((pos,) if own else ())
        e, s = call(
            functools.partial(scores_body, scale, blocks, own),
            (e_shape, s_shape),
            ins,
            dot_flops,
            held * count,
        )
        raised.append(e)
        stats.append(s)

    first = cells - len(rows)
    last = cells - 1
    f_shape = jax.ShapeDtypeStruct((8 * cells, count), f32)
    loss_shape = jax.ShapeDtypeStruct((8, BLK), f32)
    tail = BLK // 2
    head_shape = jax.ShapeDtypeStruct((held - tail, width), bf16)
    tail_shape = jax.ShapeDtypeStruct((tail, width), bf16)
    factors, g_head, w_last, lost = call(
        functools.partial(last_body, scale, blocks, cells),
        (f_shape, head_shape, w_shape, loss_shape),
        (queries, cell_rows[last], vis, *stats),
        2 * dot_flops,
        held * count,
        scratch=(pltpu.VMEM((held, count), f32),),
    )
    weights = {last: w_last}

    def gradient_of(cell, shape, added=None):
        own = cell == 0
        ins = (queries, raised[cell], factors)
        ins += ((pos,) if own else ()) + (() if added is None else (added,))
        g, w = call(
            functools.partial(gradient_body, scale, blocks, cell, own, added is not None),
            (shape, w_shape),
            ins,
            dot_flops,
        )
        weights[cell] = w
        return g

    (g_tail,) = call(
        functools.partial(tail_body, scale), (tail_shape,), (queries, w_last), dot_flops // blocks
    )
    graded = {len(rows) - 1: (g_head, g_tail)}
    for at in range(len(rows) - 1):
        cell = first + at
        g_head, g_tail, weights[cell] = call(
            functools.partial(pieces_body, scale, blocks, cell),
            (head_shape, tail_shape, w_shape),
            (queries, raised[cell], factors),
            dot_flops,
        )
        graded[at] = (g_head, g_tail)
    heads, tails = [], []
    for at, (_, back, _) in enumerate(rows):
        heads.append(lax.ppermute(graded[at][0], ("row", "col"), back))
        tails.append(lax.ppermute(graded[at][1], ("row", "col"), back))

    lost_col = sum_steps(lost, "col")
    lost_parts = from_all(lost_col, "row")

    col_back = []
    if paired:
        handed = []
        for apart in range(1, n_col // 2):
            g = gradient_of(1 + 2 * apart, g_wire)
            handed.append(lax.ppermute(g, "col", swap))
        for apart in range(1, n_col // 2):
            g = gradient_of(2 * apart, g_wire, handed[apart - 1])
            back = [(i, (i - 2 * apart) % n_col) for i in range(n_col)]
            col_back.append(lax.ppermute(g, "col", back))
        col_back.append(lax.ppermute(gradient_of(1, g_wire), "col", swap))
    else:
        for stride in range(1, n_col):
            back = [(i, (i - stride) % n_col) for i in range(n_col)]
            g = gradient_of(stride, g_wire)
            col_back.append(lax.ppermute(g, "col", back))
    g_own = gradient_of(0, g_wide)

    (toward,) = call(
        functools.partial(toward_body, scale, cells),
        (jax.ShapeDtypeStruct((count, width), f32),),
        (*[weights[cell] for cell in range(cells)], *cell_rows),
        cells * dot_flops,
    )

    wides = (g_own, *col_back)
    wire_sems = pltpu.SemaphoreType.DMA((CHUNKS,))
    rest_shape = jax.ShapeDtypeStruct((tail, width), f32)
    out_spec = pl.BlockSpec(memory_space=pl.ANY)
    written, rest = call(
        functools.partial(gather_body, len(wides)),
        (g_wide, rest_shape),
        (*wides, *heads),
        0,
        out_specs=(out_spec, whole()),
        scratch=(pltpu.VMEM((held - tail, width), f32), wire_sems),
    )
    share = 1.0 / (count * n_row * n_col)
    loss, grad_passages = call(
        functools.partial(final_body, share, len(tails), len(lost_parts)),
        (jax.ShapeDtypeStruct((1,), f32), g_wide),
        (rest, *tails, *lost_parts, written),
        0,
        out_specs=(out_spec, out_spec),
        scratch=(
            pltpu.VMEM((tail, width), f32),
            wire_sems,
            pltpu.SMEM((1,), f32),
            pltpu.SemaphoreType.DMA,
        ),
        alias=1 + len(tails) + len(lost_parts),
    )
    return (loss, toward, grad_passages)


def solution(mesh):
    return jax.shard_map(
        local_loss,
        mesh=mesh,
        in_specs=(
            P(("rep", "row", "col"), None),
            P(("rep", "row", "col"), None),
            P(("rep", "row", "col")),
            P(("rep", "row", "col"), None),
            P(("rep", "row", "col"), None),
        ),
        out_specs=(P("rep"), P(("rep", "row", "col"), None), P(("rep", "row", "col"), None)),
        check_vma=False,
    )
```

```python
import functools
import math

import jax
import jax.numpy as jnp
from jax import lax
from jax.experimental import pallas as pl
from jax.experimental.pallas import tpu as pltpu
from jax.sharding import PartitionSpec as P


BLK = 128
LOWEST = -1e30
LOG2E = math.log2(math.e)
VMEM_LIMIT = 24 << 20
CHUNKS = 2


def whole():
    return pl.BlockSpec(memory_space=pltpu.VMEM)


def call(kernel, outs, ins, flops, exps=0, out_specs=None, scratch=(), alias=None):
    moved = sum(a.size * a.dtype.itemsize for a in (*outs, *ins))
    return pl.pallas_call(
        kernel,
        out_shape=tuple(outs),
        in_specs=[
            pl.BlockSpec(memory_space=pl.ANY) if at == alias else whole() for at in range(len(ins))
        ],
        out_specs=out_specs or tuple(whole() for _ in outs),
        scratch_shapes=scratch,
        input_output_aliases={} if alias is None else {alias: len(outs) - 1},
        compiler_params=pltpu.CompilerParams(vmem_limit_bytes=VMEM_LIMIT),
        cost_estimate=pl.CostEstimate(flops=flops, bytes_accessed=moved, transcendentals=exps),
    )(*ins)


def block_stats(scores, block_at, scale):
    part = scores[block_at * BLK : (block_at + 1) * BLK]
    highest = jnp.max(part, axis=0, keepdims=True)
    raised = jnp.exp2((part - highest) * (scale * LOG2E))
    return part, highest, raised, jnp.sum(raised, axis=0, keepdims=True)


def scores_of(q_ref, p_ref):
    return lax.dot_general(
        p_ref[...], q_ref[...], (((1,), (1,)), ((), ())), preferred_element_type=jnp.float32
    )


def vis_body(blocks, col_strides, row_groups, mask_ref, roster_ref, pos_ref, out_ref):
    odd_row = (lax.axis_index("row") + lax.axis_index("col")) % 2
    odd_col = lax.axis_index("col") % 2
    height = out_ref.shape[0]
    strides = [jnp.where(odd_col == 1, odd, even) - 1 for odd, even in col_strides]
    groups = [jnp.where(odd_row == 1, odd, even) for even, odd in row_groups]
    first_row = 1 + len(strides)

    def chosen(flags_ref, columns):
        shape = (height, flags_ref.shape[0])
        cell = lax.broadcasted_iota(jnp.int32, shape, 0) // 8
        block = lax.broadcasted_iota(jnp.int32, shape, 0) % 8
        wanted = jnp.full(shape, -1, jnp.int32)
        for at, column, step in columns:
            wanted = jnp.where(cell == at, column + step * block, wanted)
        picks = lax.broadcasted_iota(jnp.int32, shape, 1) == wanted
        picks = jnp.where(picks & (block < blocks), 1.0, 0.0)
        return lax.dot_general(
            picks,
            flags_ref[...].astype(jnp.float32),
            (((1,), (0,)), ((), ())),
            preferred_element_type=jnp.float32,
        )

    masked = [(0, 0, 1)]
    masked += [(first_row + at, group * blocks, 1) for at, group in enumerate(groups)]
    seen = chosen(mask_ref, masked)
    drawn = chosen(roster_ref, [(1 + at, stride, 0) for at, stride in enumerate(strides)])
    cell = lax.broadcasted_iota(jnp.int32, seen.shape, 0) // 8
    block = lax.broadcasted_iota(jnp.int32, seen.shape, 0) % 8
    inside = block < blocks
    column = (cell >= 1) & (cell < first_row)
    held = (cell == 0) & (pos_ref[...] // BLK == block)
    visited = column & (drawn.astype(jnp.int32) == block)
    out_ref[...] = jnp.where(inside & (held | visited | (seen > 0.5)), 1.0, 0.0)


def scores_body(scale, blocks, own, *refs):
    q_ref, p_ref, pos_ref = refs[0], refs[1], refs[2]
    e_ref, stats_ref = refs[-2:]
    scores = scores_of(q_ref, p_ref)
    stats_ref[...] = jnp.zeros_like(stats_ref)
    picked = None
    for block_at in range(blocks):
        part, highest, raised, summed = block_stats(scores, block_at, scale)
        e_ref[block_at * BLK : (block_at + 1) * BLK, :] = raised
        stats_ref[block_at : block_at + 1, :] = highest * scale
        stats_ref[blocks + block_at : blocks + block_at + 1, :] = summed
        if own:
            rows = lax.broadcasted_iota(jnp.int32, part.shape, 0) + block_at * BLK
            hit = jnp.sum(jnp.where(rows == pos_ref[...], part, 0.0), axis=0, keepdims=True)
            picked = hit if picked is None else picked + hit
    if own:
        stats_ref[2 * blocks : 2 * blocks + 1, :] = picked * scale


def weights_of(e_ref, f, blocks, pos):
    parts = []
    for block_at in range(blocks):
        part = e_ref[block_at * BLK : (block_at + 1) * BLK, :] * f[block_at : block_at + 1, :]
        if pos is not None:
            rows = lax.broadcasted_iota(jnp.int32, part.shape, 0) + block_at * BLK
            part = part - jnp.where(rows == pos, 1.0, 0.0)
        parts.append(part.astype(jnp.bfloat16))
    return jnp.concatenate(parts, axis=0)


def known_body(blocks, vis_ref, *refs):
    stats_refs, out_ref = refs[:-1], refs[-1]
    seen = [vis_ref[at * 8 : at * 8 + blocks, :] > 0 for at in range(len(stats_refs))]
    tops = [
        jnp.where(flags, ref[0:blocks, :], LOWEST) for flags, ref in zip(seen, stats_refs)
    ]
    highest = None
    for top in tops:
        top = jnp.max(top, axis=0, keepdims=True)
        highest = top if highest is None else jnp.maximum(highest, top)
    total = None
    for flags, top, ref in zip(seen, tops, stats_refs):
        gap = jnp.where(flags, top - highest, LOWEST)
        part = jnp.sum(ref[blocks : 2 * blocks, :] * jnp.exp(gap), axis=0, keepdims=True)
        total = part if total is None else total + part
    out_ref[...] = jnp.zeros_like(out_ref)
    out_ref[0:1, :] = highest
    out_ref[1:2, :] = total
    out_ref[2:3, :] = stats_refs[0][2 * blocks : 2 * blocks + 1, :]


def last_body(scale, blocks, cell, q_ref, p_ref, vis_ref, known_ref, *refs):
    head_ref, w_ref, total_ref, loss_ref, e_ref = refs
    scores = scores_of(q_ref, p_ref)
    tops, sums = [], []
    for block_at in range(blocks):
        _, highest, raised, summed = block_stats(scores, block_at, scale)
        e_ref[block_at * BLK : (block_at + 1) * BLK, :] = raised
        tops.append(highest * scale)
        sums.append(summed)
    tops, sums = jnp.concatenate(tops, axis=0), jnp.concatenate(sums, axis=0)
    seen = vis_ref[cell * 8 : cell * 8 + blocks, :] > 0
    tops = jnp.where(seen, tops, LOWEST)
    known = known_ref[0:1, :]
    highest = jnp.maximum(known, jnp.max(tops, axis=0, keepdims=True))
    here = sums * jnp.exp(jnp.where(seen, tops - highest, LOWEST))
    total = known_ref[1:2, :] * jnp.exp(known - highest) + jnp.sum(here, axis=0, keepdims=True)
    log_total = highest + jnp.log(total)
    factor = jnp.exp(jnp.where(seen, tops - log_total, LOWEST))
    total_ref[...] = jnp.broadcast_to(log_total, total_ref.shape)
    lost = jnp.sum(log_total - known_ref[2:3, :], axis=1, keepdims=True)
    loss_ref[...] = jnp.broadcast_to(lost, loss_ref.shape)
    weights = weights_of(e_ref, factor, blocks, None)
    w_ref[...] = weights
    put_pieces((head_ref,), weights, q_ref, scale)


def factors_body(blocks, vis_ref, total_ref, *refs):
    stats_refs, f_ref = refs[:-1], refs[-1]
    f_ref[...] = jnp.zeros_like(f_ref)
    log_total = total_ref[0:1, :]
    for cell, ref in enumerate(stats_refs):
        seen = vis_ref[cell * 8 : cell * 8 + blocks, :] > 0
        gap = jnp.where(seen, ref[0:blocks, :] - log_total, LOWEST)
        f_ref[cell * 8 : cell * 8 + blocks, :] = jnp.exp(gap)


def put_pieces(pieces, weights, q_ref, scale):
    at = 0
    for ref in pieces:
        part = weights[at : at + ref.shape[0]]
        gradient = jnp.dot(part, q_ref[...], preferred_element_type=jnp.float32) * scale
        ref[...] = gradient.astype(ref.dtype)
        at += ref.shape[0]


def tail_body(scale, q_ref, w_ref, tail_ref):
    part = w_ref[w_ref.shape[0] - tail_ref.shape[0] :, :]
    gradient = jnp.dot(part, q_ref[...], preferred_element_type=jnp.float32) * scale
    tail_ref[...] = gradient.astype(tail_ref.dtype)


def pieces_body(scale, blocks, cell, q_ref, e_ref, f_ref, head_ref, tail_ref, w_ref):
    weights = weights_of(e_ref, f_ref[cell * 8 : cell * 8 + 8, :], blocks, None)
    w_ref[...] = weights
    put_pieces((head_ref, tail_ref), weights, q_ref, scale)


def gradient_body(scale, blocks, cell, own, added, *refs):
    refs = list(refs)
    q_ref, e_ref, f_ref = refs[:3]
    del refs[:3]
    pos = refs.pop(0)[...] if own else None
    more_ref = refs.pop(0) if added else None
    g_ref, w_ref = refs
    weights = weights_of(e_ref, f_ref[cell * 8 : cell * 8 + 8, :], blocks, pos)
    w_ref[...] = weights
    gradient = jnp.dot(weights, q_ref[...], preferred_element_type=jnp.float32) * scale
    if added:
        gradient = gradient + more_ref[...].astype(jnp.float32)
    g_ref[...] = gradient.astype(g_ref.dtype)


def toward_body(scale, cells, *refs):
    w_refs, p_refs, out_ref = refs[:cells], refs[cells : 2 * cells], refs[2 * cells]
    total = None
    for w_ref, p_ref in zip(w_refs, p_refs):
        part = lax.dot_general(
            w_ref[...], p_ref[...], (((0,), (0,)), ((), ())), preferred_element_type=jnp.float32
        )
        total = part if total is None else total + part
    out_ref[...] = total * scale


def gather_body(wholes, *refs):
    out_ref, rest_ref, held_ref, sem = refs[-4:]
    heads = refs[wholes:-4]
    chunk = held_ref.shape[0] // CHUNKS
    copies = []
    for at in range(CHUNKS):
        rows = pl.ds(at * chunk, chunk)
        total = refs[0][rows, :]
        for ref in (*refs[1:wholes], *heads):
            total = total + ref[rows, :].astype(jnp.float32)
        held_ref[rows, :] = total
        copy = pltpu.make_async_copy(held_ref.at[rows, :], out_ref.at[rows, :], sem.at[at])
        copy.start()
        copies.append(copy)
    rows = pl.ds(held_ref.shape[0], rest_ref.shape[0])
    total = refs[0][rows, :]
    for ref in refs[1:wholes]:
        total = total + ref[rows, :].astype(jnp.float32)
    rest_ref[...] = total
    for copy in copies:
        copy.wait()


def final_body(share, tails, parts, rest_ref, *refs):
    tail_refs, lost_refs = refs[:tails], refs[tails : tails + parts]
    loss_ref, out_ref, held_ref, sem, loss_sm, loss_sem = refs[tails + parts + 1 :]
    total = lost_refs[0][...]
    for ref in lost_refs[1:]:
        total = total + ref[...]
    loss_sm[0] = jnp.max(total) * share
    copies = [pltpu.make_async_copy(loss_sm, loss_ref, loss_sem)]
    copies[0].start()
    first = out_ref.shape[0] - held_ref.shape[0]
    chunk = held_ref.shape[0] // CHUNKS
    for at in range(CHUNKS):
        rows = pl.ds(at * chunk, chunk)
        total = rest_ref[rows, :]
        for ref in tail_refs:
            total = total + ref[rows, :].astype(jnp.float32)
        held_ref[rows, :] = total
        there = out_ref.at[pl.ds(first + at * chunk, chunk), :]
        copy = pltpu.make_async_copy(held_ref.at[rows, :], there, sem.at[at])
        copy.start()
        copies.append(copy)
    for copy in copies:
        copy.wait()


def row_plan(n_row, n_col, reach):
    cells = [(r, c) for r in range(n_row) for c in range(n_col)]

    def pairs(partner):
        return [(r * n_col + c, partner(r, c) % n_row * n_col + c) for r, c in cells]

    if reach == 1 and n_row % 2 == 0:
        first = pairs(lambda r, c: r + 1 if (r + c) % 2 == 0 else r - 1)
        second = pairs(lambda r, c: r - 1 if (r + c) % 2 == 0 else r + 1)
        return [(first, first, (2, 1)), (second, second, (1, 2))]
    plan = []
    offsets = list(range(-reach, 0)) + list(range(1, reach + 1))
    for group_at, offset in enumerate(offsets):
        there = pairs(lambda r, c: r - offset)
        back = pairs(lambda r, c: r + offset)
        plan.append((there, back, (group_at + 1, group_at + 1)))
    return plan


def sum_steps(array, axis):
    size = lax.axis_size(axis)
    if size & (size - 1):
        return lax.psum(array, axis)
    step = 1
    while step < size:
        pairs = [(i, i ^ step) for i in range(size)]
        array = array + lax.ppermute(array, axis, pairs)
        step *= 2
    return array


def partners(size, step):
    if size & (size - 1):
        return [(i, (i + step) % size) for i in range(size)]
    return [(i, i ^ step) for i in range(size)]


def from_all(array, axis):
    size = lax.axis_size(axis)
    if size > 4:
        return [sum_steps(array, axis)]
    shifts = range(1, size)
    return [array] + [lax.ppermute(array, axis, partners(size, s)) for s in shifts]


def local_loss(queries, passages, positive, block_mask, roster):
    n_row = lax.axis_size("row")
    n_col = lax.axis_size("col")
    reach = min(2, (n_row - 1) // 2)
    count, width = queries.shape
    held = passages.shape[0]
    blocks = held // BLK
    scale = width ** (-0.5)
    f32, bf16 = jnp.float32, jnp.bfloat16

    rows = row_plan(n_row, n_col, reach)
    near = [lax.ppermute(passages, ("row", "col"), there) for there, _, _ in rows]

    swap = [(i, i ^ 1) for i in range(n_col)]
    col_cells = []
    paired = n_col % 2 == 0
    if paired:
        col_cells.append((lax.ppermute(passages, "col", swap), 1, n_col - 1))
        for apart in range(1, n_col // 2):
            there = [(i, (i + 2 * apart) % n_col) for i in range(n_col)]
            far = lax.ppermute(passages, "col", there)
            cross = lax.ppermute(far, "col", swap)
            col_cells.append((far, 2 * apart, 2 * apart))
            col_cells.append((cross, 2 * apart + 1, 2 * apart - 1))
    else:
        for stride in range(1, n_col):
            there = [(i, (i + stride) % n_col) for i in range(n_col)]
            far = lax.ppermute(passages, "col", there)
            col_cells.append((far, stride, stride))

    pos = positive.reshape(1, count)
    (vis,) = call(
        functools.partial(
            vis_body,
            blocks,
            [(odd, even) for _, odd, even in col_cells],
            [groups for _, _, groups in rows],
        ),
        (jax.ShapeDtypeStruct((8 * (1 + len(col_cells) + len(rows)), count), f32),),
        (block_mask.T, roster.T, pos),
        0,
    )

    cell_rows = [passages] + [cell[0] for cell in col_cells] + near
    cells = len(cell_rows)
    e_shape = jax.ShapeDtypeStruct((held, count), f32)
    w_shape = jax.ShapeDtypeStruct((held, count), bf16)
    s_shape = jax.ShapeDtypeStruct((8, count), f32)
    g_wire = jax.ShapeDtypeStruct((held, width), bf16)
    g_wide = jax.ShapeDtypeStruct((held, width), f32)
    dot_flops = 2 * held * count * width

    raised, stats = [], []
    for cell in range(cells - 1):
        own = cell == 0
        ins = (queries, cell_rows[cell]) + ((pos,) if own else ())
        e, s = call(
            functools.partial(scores_body, scale, blocks, own),
            (e_shape, s_shape),
            ins,
            dot_flops,
            held * count,
        )
        raised.append(e)
        stats.append(s)

    first = cells - len(rows)
    last = cells - 1
    f_shape = jax.ShapeDtypeStruct((8 * cells, count), f32)
    loss_shape = jax.ShapeDtypeStruct((8, BLK), f32)
    tail = BLK // 2
    head_shape = jax.ShapeDtypeStruct((held - tail, width), bf16)
    tail_shape = jax.ShapeDtypeStruct((tail, width), bf16)
    (known,) = call(functools.partial(known_body, blocks), (s_shape,), (vis, *stats), 0)
    g_head, w_last, log_total, lost = call(
        functools.partial(last_body, scale, blocks, last),
        (head_shape, w_shape, s_shape, loss_shape),
        (queries, cell_rows[last], vis, known),
        2 * dot_flops,
        held * count,
        scratch=(pltpu.VMEM((held, count), f32),),
    )
    (factors,) = call(
        functools.partial(factors_body, blocks), (f_shape,), (vis, log_total, *stats), 0
    )
    weights = {last: w_last}

    def gradient_of(cell, shape, added=None):
        own = cell == 0
        ins = (queries, raised[cell], factors)
        ins += ((pos,) if own else ()) + (() if added is None else (added,))
        g, w = call(
            functools.partial(gradient_body, scale, blocks, cell, own, added is not None),
            (shape, w_shape),
            ins,
            dot_flops,
        )
        weights[cell] = w
        return g

    (g_tail,) = call(
        functools.partial(tail_body, scale), (tail_shape,), (queries, w_last), dot_flops // blocks
    )
    graded = {len(rows) - 1: (g_head, g_tail)}
    for at in range(len(rows) - 1):
        cell = first + at
        g_head, g_tail, weights[cell] = call(
            functools.partial(pieces_body, scale, blocks, cell),
            (head_shape, tail_shape, w_shape),
            (queries, raised[cell], factors),
            dot_flops,
        )
        graded[at] = (g_head, g_tail)
    heads, tails = [], []
    for at, (_, back, _) in enumerate(rows):
        heads.append(lax.ppermute(graded[at][0], ("row", "col"), back))
        tails.append(lax.ppermute(graded[at][1], ("row", "col"), back))

    lost_col = sum_steps(lost, "col")
    lost_parts = from_all(lost_col, "row")

    col_back = []
    if paired:
        handed = []
        for apart in range(1, n_col // 2):
            g = gradient_of(1 + 2 * apart, g_wire)
            handed.append(lax.ppermute(g, "col", swap))
        for apart in range(1, n_col // 2):
            g = gradient_of(2 * apart, g_wire, handed[apart - 1])
            back = [(i, (i - 2 * apart) % n_col) for i in range(n_col)]
            col_back.append(lax.ppermute(g, "col", back))
        col_back.append(lax.ppermute(gradient_of(1, g_wire), "col", swap))
    else:
        for stride in range(1, n_col):
            back = [(i, (i - stride) % n_col) for i in range(n_col)]
            g = gradient_of(stride, g_wire)
            col_back.append(lax.ppermute(g, "col", back))
    g_own = gradient_of(0, g_wide)

    (toward,) = call(
        functools.partial(toward_body, scale, cells),
        (jax.ShapeDtypeStruct((count, width), f32),),
        (*[weights[cell] for cell in range(cells)], *cell_rows),
        cells * dot_flops,
    )

    wides = (g_own, *col_back)
    wire_sems = pltpu.SemaphoreType.DMA((CHUNKS,))
    rest_shape = jax.ShapeDtypeStruct((tail, width), f32)
    out_spec = pl.BlockSpec(memory_space=pl.ANY)
    written, rest = call(
        functools.partial(gather_body, len(wides)),
        (g_wide, rest_shape),
        (*wides, *heads),
        0,
        out_specs=(out_spec, whole()),
        scratch=(pltpu.VMEM((held - tail, width), f32), wire_sems),
    )
    share = 1.0 / (count * n_row * n_col)
    loss, grad_passages = call(
        functools.partial(final_body, share, len(tails), len(lost_parts)),
        (jax.ShapeDtypeStruct((1,), f32), g_wide),
        (rest, *tails, *lost_parts, written),
        0,
        out_specs=(out_spec, out_spec),
        scratch=(
            pltpu.VMEM((tail, width), f32),
            wire_sems,
            pltpu.SMEM((1,), f32),
            pltpu.SemaphoreType.DMA,
        ),
        alias=1 + len(tails) + len(lost_parts),
    )
    return (loss, toward, grad_passages)


def solution(mesh):
    return jax.shard_map(
        local_loss,
        mesh=mesh,
        in_specs=(
            P(("rep", "row", "col"), None),
            P(("rep", "row", "col"), None),
            P(("rep", "row", "col")),
            P(("rep", "row", "col"), None),
            P(("rep", "row", "col"), None),
        ),
        out_specs=(P("rep"), P(("rep", "row", "col"), None), P(("rep", "row", "col"), None)),
        check_vma=False,
    )
```

```python
import functools
import math

import jax
import jax.numpy as jnp
from jax import lax
from jax.experimental import pallas as pl
from jax.experimental.pallas import tpu as pltpu
from jax.sharding import PartitionSpec as P


BLK = 128
LOWEST = -1e30
LOG2E = math.log2(math.e)
VMEM_LIMIT = 24 << 20
CHUNKS = 2


def whole():
    return pl.BlockSpec(memory_space=pltpu.VMEM)


def call(kernel, outs, ins, flops, exps=0, out_specs=None, scratch=(), alias=None):
    moved = sum(a.size * a.dtype.itemsize for a in (*outs, *ins))
    return pl.pallas_call(
        kernel,
        out_shape=tuple(outs),
        in_specs=[
            pl.BlockSpec(memory_space=pl.ANY) if at == alias else whole() for at in range(len(ins))
        ],
        out_specs=out_specs or tuple(whole() for _ in outs),
        scratch_shapes=scratch,
        input_output_aliases={} if alias is None else {alias: len(outs) - 1},
        compiler_params=pltpu.CompilerParams(vmem_limit_bytes=VMEM_LIMIT),
        cost_estimate=pl.CostEstimate(flops=flops, bytes_accessed=moved, transcendentals=exps),
    )(*ins)


def block_stats(scores, block_at, scale):
    part = scores[block_at * BLK : (block_at + 1) * BLK]
    highest = jnp.max(part, axis=0, keepdims=True)
    raised = jnp.exp2((part - highest) * (scale * LOG2E))
    return part, highest, raised, jnp.sum(raised, axis=0, keepdims=True)


def scores_of(q_ref, p_ref):
    return lax.dot_general(
        p_ref[...], q_ref[...], (((1,), (1,)), ((), ())), preferred_element_type=jnp.float32
    )


def vis_body(blocks, col_strides, row_groups, mask_ref, roster_ref, pos_ref, out_ref):
    odd_row = (lax.axis_index("row") + lax.axis_index("col")) % 2
    odd_col = lax.axis_index("col") % 2
    height = out_ref.shape[0]
    strides = [jnp.where(odd_col == 1, odd, even) - 1 for odd, even in col_strides]
    groups = [jnp.where(odd_row == 1, odd, even) for even, odd in row_groups]
    first_row = 1 + len(strides)

    def chosen(flags_ref, columns):
        shape = (height, flags_ref.shape[0])
        cell = lax.broadcasted_iota(jnp.int32, shape, 0) // 8
        block = lax.broadcasted_iota(jnp.int32, shape, 0) % 8
        wanted = jnp.full(shape, -1, jnp.int32)
        for at, column, step in columns:
            wanted = jnp.where(cell == at, column + step * block, wanted)
        picks = lax.broadcasted_iota(jnp.int32, shape, 1) == wanted
        picks = jnp.where(picks & (block < blocks), 1.0, 0.0)
        return lax.dot_general(
            picks,
            flags_ref[...].astype(jnp.float32),
            (((1,), (0,)), ((), ())),
            preferred_element_type=jnp.float32,
        )

    masked = [(0, 0, 1)]
    masked += [(first_row + at, group * blocks, 1) for at, group in enumerate(groups)]
    seen = chosen(mask_ref, masked)
    drawn = chosen(roster_ref, [(1 + at, stride, 0) for at, stride in enumerate(strides)])
    cell = lax.broadcasted_iota(jnp.int32, seen.shape, 0) // 8
    block = lax.broadcasted_iota(jnp.int32, seen.shape, 0) % 8
    inside = block < blocks
    column = (cell >= 1) & (cell < first_row)
    held = (cell == 0) & (pos_ref[...] // BLK == block)
    visited = column & (drawn.astype(jnp.int32) == block)
    out_ref[...] = jnp.where(inside & (held | visited | (seen > 0.5)), 1.0, 0.0)


def scores_body(scale, blocks, own, *refs):
    q_ref, p_ref, pos_ref = refs[0], refs[1], refs[2]
    e_ref, stats_ref = refs[-2:]
    scores = scores_of(q_ref, p_ref)
    stats_ref[...] = jnp.zeros_like(stats_ref)
    picked = None
    for block_at in range(blocks):
        part, highest, raised, summed = block_stats(scores, block_at, scale)
        e_ref[block_at * BLK : (block_at + 1) * BLK, :] = raised
        stats_ref[block_at : block_at + 1, :] = highest * scale
        stats_ref[blocks + block_at : blocks + block_at + 1, :] = summed
        if own:
            rows = lax.broadcasted_iota(jnp.int32, part.shape, 0) + block_at * BLK
            hit = jnp.sum(jnp.where(rows == pos_ref[...], part, 0.0), axis=0, keepdims=True)
            picked = hit if picked is None else picked + hit
    if own:
        stats_ref[2 * blocks : 2 * blocks + 1, :] = picked * scale


def weights_of(e_ref, f, blocks, pos):
    parts = []
    for block_at in range(blocks):
        part = e_ref[block_at * BLK : (block_at + 1) * BLK, :] * f[block_at : block_at + 1, :]
        if pos is not None:
            rows = lax.broadcasted_iota(jnp.int32, part.shape, 0) + block_at * BLK
            part = part - jnp.where(rows == pos, 1.0, 0.0)
        parts.append(part.astype(jnp.bfloat16))
    return jnp.concatenate(parts, axis=0)


def known_body(blocks, vis_ref, *refs):
    stats_refs, out_ref = refs[:-1], refs[-1]
    seen = [vis_ref[at * 8 : at * 8 + blocks, :] > 0 for at in range(len(stats_refs))]
    tops = [
        jnp.where(flags, ref[0:blocks, :], LOWEST) for flags, ref in zip(seen, stats_refs)
    ]
    highest = None
    for top in tops:
        top = jnp.max(top, axis=0, keepdims=True)
        highest = top if highest is None else jnp.maximum(highest, top)
    total = None
    for flags, top, ref in zip(seen, tops, stats_refs):
        gap = jnp.where(flags, top - highest, LOWEST)
        part = jnp.sum(ref[blocks : 2 * blocks, :] * jnp.exp(gap), axis=0, keepdims=True)
        total = part if total is None else total + part
    out_ref[...] = jnp.zeros_like(out_ref)
    out_ref[0:1, :] = highest
    out_ref[1:2, :] = total
    out_ref[2:3, :] = stats_refs[0][2 * blocks : 2 * blocks + 1, :]


def last_body(scale, blocks, cell, q_ref, p_ref, vis_ref, known_ref, *refs):
    head_ref, w_ref, total_ref, e_ref = refs
    scores = scores_of(q_ref, p_ref)
    tops, sums = [], []
    for block_at in range(blocks):
        _, highest, raised, summed = block_stats(scores, block_at, scale)
        e_ref[block_at * BLK : (block_at + 1) * BLK, :] = raised
        tops.append(highest * scale)
        sums.append(summed)
    tops, sums = jnp.concatenate(tops, axis=0), jnp.concatenate(sums, axis=0)
    seen = vis_ref[cell * 8 : cell * 8 + blocks, :] > 0
    tops = jnp.where(seen, tops, LOWEST)
    known = known_ref[0:1, :]
    highest = jnp.maximum(known, jnp.max(tops, axis=0, keepdims=True))
    here = sums * jnp.exp(jnp.where(seen, tops - highest, LOWEST))
    total = known_ref[1:2, :] * jnp.exp(known - highest) + jnp.sum(here, axis=0, keepdims=True)
    log_total = highest + jnp.log(total)
    factor = jnp.exp(jnp.where(seen, tops - log_total, LOWEST))
    total_ref[...] = jnp.broadcast_to(log_total, total_ref.shape)
    weights = weights_of(e_ref, factor, blocks, None)
    w_ref[...] = weights
    put_pieces((head_ref,), weights, q_ref, scale)


def factors_body(blocks, vis_ref, total_ref, known_ref, *refs):
    stats_refs, f_ref, loss_ref = refs[:-2], refs[-2], refs[-1]
    f_ref[...] = jnp.zeros_like(f_ref)
    log_total = total_ref[0:1, :]
    lost = jnp.sum(log_total - known_ref[2:3, :], axis=1, keepdims=True)
    loss_ref[...] = jnp.broadcast_to(lost, loss_ref.shape)
    for cell, ref in enumerate(stats_refs):
        seen = vis_ref[cell * 8 : cell * 8 + blocks, :] > 0
        gap = jnp.where(seen, ref[0:blocks, :] - log_total, LOWEST)
        f_ref[cell * 8 : cell * 8 + blocks, :] = jnp.exp(gap)


def put_pieces(pieces, weights, q_ref, scale):
    at = 0
    for ref in pieces:
        part = weights[at : at + ref.shape[0]]
        gradient = jnp.dot(part, q_ref[...], preferred_element_type=jnp.float32) * scale
        ref[...] = gradient.astype(ref.dtype)
        at += ref.shape[0]


def tail_body(scale, q_ref, w_ref, tail_ref):
    part = w_ref[w_ref.shape[0] - tail_ref.shape[0] :, :]
    gradient = jnp.dot(part, q_ref[...], preferred_element_type=jnp.float32) * scale
    tail_ref[...] = gradient.astype(tail_ref.dtype)


def pieces_body(scale, blocks, cell, q_ref, e_ref, f_ref, head_ref, tail_ref, w_ref):
    weights = weights_of(e_ref, f_ref[cell * 8 : cell * 8 + 8, :], blocks, None)
    w_ref[...] = weights
    put_pieces((head_ref, tail_ref), weights, q_ref, scale)


def gradient_body(scale, blocks, cell, own, added, *refs):
    refs = list(refs)
    q_ref, e_ref, f_ref = refs[:3]
    del refs[:3]
    pos = refs.pop(0)[...] if own else None
    more_ref = refs.pop(0) if added else None
    g_ref, w_ref = refs
    weights = weights_of(e_ref, f_ref[cell * 8 : cell * 8 + 8, :], blocks, pos)
    w_ref[...] = weights
    gradient = jnp.dot(weights, q_ref[...], preferred_element_type=jnp.float32) * scale
    if added:
        gradient = gradient + more_ref[...].astype(jnp.float32)
    g_ref[...] = gradient.astype(g_ref.dtype)


def toward_body(scale, cells, *refs):
    w_refs, p_refs, out_ref = refs[:cells], refs[cells : 2 * cells], refs[2 * cells]
    total = None
    for w_ref, p_ref in zip(w_refs, p_refs):
        part = lax.dot_general(
            w_ref[...], p_ref[...], (((0,), (0,)), ((), ())), preferred_element_type=jnp.float32
        )
        total = part if total is None else total + part
    out_ref[...] = total * scale


def gather_body(wholes, *refs):
    out_ref, rest_ref, held_ref, sem = refs[-4:]
    heads = refs[wholes:-4]
    chunk = held_ref.shape[0] // CHUNKS
    copies = []
    for at in range(CHUNKS):
        rows = pl.ds(at * chunk, chunk)
        total = refs[0][rows, :]
        for ref in (*refs[1:wholes], *heads):
            total = total + ref[rows, :].astype(jnp.float32)
        held_ref[rows, :] = total
        copy = pltpu.make_async_copy(held_ref.at[rows, :], out_ref.at[rows, :], sem.at[at])
        copy.start()
        copies.append(copy)
    rows = pl.ds(held_ref.shape[0], rest_ref.shape[0])
    total = refs[0][rows, :]
    for ref in refs[1:wholes]:
        total = total + ref[rows, :].astype(jnp.float32)
    rest_ref[...] = total
    for copy in copies:
        copy.wait()


def final_body(share, tails, parts, rest_ref, *refs):
    tail_refs, lost_refs = refs[:tails], refs[tails : tails + parts]
    loss_ref, out_ref, held_ref, sem, loss_sm, loss_sem = refs[tails + parts + 1 :]
    total = lost_refs[0][...]
    for ref in lost_refs[1:]:
        total = total + ref[...]
    loss_sm[0] = jnp.max(total) * share
    copies = [pltpu.make_async_copy(loss_sm, loss_ref, loss_sem)]
    copies[0].start()
    first = out_ref.shape[0] - held_ref.shape[0]
    chunk = held_ref.shape[0] // CHUNKS
    for at in range(CHUNKS):
        rows = pl.ds(at * chunk, chunk)
        total = rest_ref[rows, :]
        for ref in tail_refs:
            total = total + ref[rows, :].astype(jnp.float32)
        held_ref[rows, :] = total
        there = out_ref.at[pl.ds(first + at * chunk, chunk), :]
        copy = pltpu.make_async_copy(held_ref.at[rows, :], there, sem.at[at])
        copy.start()
        copies.append(copy)
    for copy in copies:
        copy.wait()


def row_plan(n_row, n_col, reach):
    cells = [(r, c) for r in range(n_row) for c in range(n_col)]

    def pairs(partner):
        return [(r * n_col + c, partner(r, c) % n_row * n_col + c) for r, c in cells]

    if reach == 1 and n_row % 2 == 0:
        first = pairs(lambda r, c: r + 1 if (r + c) % 2 == 0 else r - 1)
        second = pairs(lambda r, c: r - 1 if (r + c) % 2 == 0 else r + 1)
        return [(first, first, (2, 1)), (second, second, (1, 2))]
    plan = []
    offsets = list(range(-reach, 0)) + list(range(1, reach + 1))
    for group_at, offset in enumerate(offsets):
        there = pairs(lambda r, c: r - offset)
        back = pairs(lambda r, c: r + offset)
        plan.append((there, back, (group_at + 1, group_at + 1)))
    return plan


def sum_steps(array, axis):
    size = lax.axis_size(axis)
    if size & (size - 1):
        return lax.psum(array, axis)
    step = 1
    while step < size:
        pairs = [(i, i ^ step) for i in range(size)]
        array = array + lax.ppermute(array, axis, pairs)
        step *= 2
    return array


def partners(size, step):
    if size & (size - 1):
        return [(i, (i + step) % size) for i in range(size)]
    return [(i, i ^ step) for i in range(size)]


def from_all(array, axis):
    size = lax.axis_size(axis)
    if size > 4:
        return [sum_steps(array, axis)]
    shifts = range(1, size)
    return [array] + [lax.ppermute(array, axis, partners(size, s)) for s in shifts]


def local_loss(queries, passages, positive, block_mask, roster):
    n_row = lax.axis_size("row")
    n_col = lax.axis_size("col")
    reach = min(2, (n_row - 1) // 2)
    count, width = queries.shape
    held = passages.shape[0]
    blocks = held // BLK
    scale = width ** (-0.5)
    f32, bf16 = jnp.float32, jnp.bfloat16

    rows = row_plan(n_row, n_col, reach)
    near = [lax.ppermute(passages, ("row", "col"), there) for there, _, _ in rows]

    swap = [(i, i ^ 1) for i in range(n_col)]
    col_cells = []
    paired = n_col % 2 == 0
    if paired:
        col_cells.append((lax.ppermute(passages, "col", swap), 1, n_col - 1))
        for apart in range(1, n_col // 2):
            there = [(i, (i + 2 * apart) % n_col) for i in range(n_col)]
            far = lax.ppermute(passages, "col", there)
            cross = lax.ppermute(far, "col", swap)
            col_cells.append((far, 2 * apart, 2 * apart))
            col_cells.append((cross, 2 * apart + 1, 2 * apart - 1))
    else:
        for stride in range(1, n_col):
            there = [(i, (i + stride) % n_col) for i in range(n_col)]
            far = lax.ppermute(passages, "col", there)
            col_cells.append((far, stride, stride))

    pos = positive.reshape(1, count)
    (vis,) = call(
        functools.partial(
            vis_body,
            blocks,
            [(odd, even) for _, odd, even in col_cells],
            [groups for _, _, groups in rows],
        ),
        (jax.ShapeDtypeStruct((8 * (1 + len(col_cells) + len(rows)), count), f32),),
        (block_mask.T, roster.T, pos),
        0,
    )

    cell_rows = [passages] + [cell[0] for cell in col_cells] + near
    cells = len(cell_rows)
    e_shape = jax.ShapeDtypeStruct((held, count), f32)
    w_shape = jax.ShapeDtypeStruct((held, count), bf16)
    s_shape = jax.ShapeDtypeStruct((8, count), f32)
    g_wire = jax.ShapeDtypeStruct((held, width), bf16)
    g_wide = jax.ShapeDtypeStruct((held, width), f32)
    dot_flops = 2 * held * count * width

    raised, stats = [], []
    for cell in range(cells - 1):
        own = cell == 0
        ins = (queries, cell_rows[cell]) + ((pos,) if own else ())
        e, s = call(
            functools.partial(scores_body, scale, blocks, own),
            (e_shape, s_shape),
            ins,
            dot_flops,
            held * count,
        )
        raised.append(e)
        stats.append(s)

    first = cells - len(rows)
    last = cells - 1
    f_shape = jax.ShapeDtypeStruct((8 * cells, count), f32)
    loss_shape = jax.ShapeDtypeStruct((8, BLK), f32)
    tail = BLK // 2
    head_shape = jax.ShapeDtypeStruct((held - tail, width), bf16)
    tail_shape = jax.ShapeDtypeStruct((tail, width), bf16)
    (known,) = call(functools.partial(known_body, blocks), (s_shape,), (vis, *stats), 0)
    g_head, w_last, log_total = call(
        functools.partial(last_body, scale, blocks, last),
        (head_shape, w_shape, s_shape),
        (queries, cell_rows[last], vis, known),
        2 * dot_flops,
        held * count,
        scratch=(pltpu.VMEM((held, count), f32),),
    )
    factors, lost = call(
        functools.partial(factors_body, blocks),
        (f_shape, loss_shape),
        (vis, log_total, known, *stats),
        0,
    )
    weights = {last: w_last}

    def gradient_of(cell, shape, added=None):
        own = cell == 0
        ins = (queries, raised[cell], factors)
        ins += ((pos,) if own else ()) + (() if added is None else (added,))
        g, w = call(
            functools.partial(gradient_body, scale, blocks, cell, own, added is not None),
            (shape, w_shape),
            ins,
            dot_flops,
        )
        weights[cell] = w
        return g

    (g_tail,) = call(
        functools.partial(tail_body, scale), (tail_shape,), (queries, w_last), dot_flops // blocks
    )
    graded = {len(rows) - 1: (g_head, g_tail)}
    for at in range(len(rows) - 1):
        cell = first + at
        g_head, g_tail, weights[cell] = call(
            functools.partial(pieces_body, scale, blocks, cell),
            (head_shape, tail_shape, w_shape),
            (queries, raised[cell], factors),
            dot_flops,
        )
        graded[at] = (g_head, g_tail)
    heads, tails = [], []
    for at, (_, back, _) in enumerate(rows):
        heads.append(lax.ppermute(graded[at][0], ("row", "col"), back))
        tails.append(lax.ppermute(graded[at][1], ("row", "col"), back))

    lost_col = sum_steps(lost, "col")
    lost_parts = from_all(lost_col, "row")

    col_back = []
    if paired:
        handed = []
        for apart in range(1, n_col // 2):
            g = gradient_of(1 + 2 * apart, g_wire)
            handed.append(lax.ppermute(g, "col", swap))
        for apart in range(1, n_col // 2):
            g = gradient_of(2 * apart, g_wire, handed[apart - 1])
            back = [(i, (i - 2 * apart) % n_col) for i in range(n_col)]
            col_back.append(lax.ppermute(g, "col", back))
        col_back.append(lax.ppermute(gradient_of(1, g_wire), "col", swap))
    else:
        for stride in range(1, n_col):
            back = [(i, (i - stride) % n_col) for i in range(n_col)]
            g = gradient_of(stride, g_wire)
            col_back.append(lax.ppermute(g, "col", back))
    g_own = gradient_of(0, g_wide)

    (toward,) = call(
        functools.partial(toward_body, scale, cells),
        (jax.ShapeDtypeStruct((count, width), f32),),
        (*[weights[cell] for cell in range(cells)], *cell_rows),
        cells * dot_flops,
    )

    wides = (g_own, *col_back)
    wire_sems = pltpu.SemaphoreType.DMA((CHUNKS,))
    rest_shape = jax.ShapeDtypeStruct((tail, width), f32)
    out_spec = pl.BlockSpec(memory_space=pl.ANY)
    written, rest = call(
        functools.partial(gather_body, len(wides)),
        (g_wide, rest_shape),
        (*wides, *heads),
        0,
        out_specs=(out_spec, whole()),
        scratch=(pltpu.VMEM((held - tail, width), f32), wire_sems),
    )
    share = 1.0 / (count * n_row * n_col)
    loss, grad_passages = call(
        functools.partial(final_body, share, len(tails), len(lost_parts)),
        (jax.ShapeDtypeStruct((1,), f32), g_wide),
        (rest, *tails, *lost_parts, written),
        0,
        out_specs=(out_spec, out_spec),
        scratch=(
            pltpu.VMEM((tail, width), f32),
            wire_sems,
            pltpu.SMEM((1,), f32),
            pltpu.SemaphoreType.DMA,
        ),
        alias=1 + len(tails) + len(lost_parts),
    )
    return (loss, toward, grad_passages)


def solution(mesh):
    return jax.shard_map(
        local_loss,
        mesh=mesh,
        in_specs=(
            P(("rep", "row", "col"), None),
            P(("rep", "row", "col"), None),
            P(("rep", "row", "col")),
            P(("rep", "row", "col"), None),
            P(("rep", "row", "col"), None),
        ),
        out_specs=(P("rep"), P(("rep", "row", "col"), None), P(("rep", "row", "col"), None)),
        check_vma=False,
    )
```
